32 devices in a mesh: groups: 2 (over x), fsdp: 16 (over z, y, core).
Axes of the slice: x: 2, y: 2, z: 4, core: 2. Of those that a mesh axis runs over, the one named last changes fastest.
Arguments:
- obs_feat: bfloat16 [12288, 2048], P(('groups', 'fsdp')), parts along dimension 0, may hold values from -6 to 6
- reward: float32 [512, 24], P(('groups', 'fsdp')), parts along dimension 0, may hold values from -22 to 22
- value_old: float32 [512, 25], P(('groups', 'fsdp')), parts along dimension 0, may hold values from -6 to 6
- done: int32 [512, 24], P(('groups', 'fsdp')), parts along dimension 0, may hold values 0 or 1
- minibatch_perm: int32 [12288], P(('groups', 'fsdp')), parts along dimension 0, may hold values from 0 to 6143, as said below
- old_mean: bfloat16 [12288, 12], P(('groups', 'fsdp')), parts along dimension 0, may hold values from -6 to 6
- noise: bfloat16 [12288, 12], P(('groups', 'fsdp')), parts along dimension 0, may hold values from -6 to 6
- gain_in: float32 [2048], replicated, may hold values from 0.5 to 1.5
- out_weight: bfloat16 [2048, 2048], P('fsdp'), may hold values from -0.125 to 0.125
- head_weight: bfloat16 [2048, 13], replicated, may hold values from -0.125 to 0.125
- log_std: float32 [12], replicated, may hold values from 0.7 to 1.3
Outputs:
- hidden_out: bfloat16 [12288, 2048], P(('groups', 'fsdp')), parts along dimension 0
- grad_weight: float32 [4096, 2048], P(('groups', 'fsdp')), parts along dimension 0
- grad_head: float32 [4096, 13], P('groups'), parts along dimension 0
- grad_std: float32 [24], P('groups'), parts along dimension 0
The draws below stay inside these ranges and needn't reach their ends.
There are 2 independent parts, one for each index of `groups`. The reference program is written for one: setup_inputs(seed, part) draws one part's arguments, and reference() takes and returns one part's arrays. A program takes and returns all parts, laid end to end along the dimension named above; an argument that names none is the same for every part. Nothing has to cross between parts.
Inputs may be any that keep to these rules, and one draw needn't show every extreme that they name: `minibatch_perm`: rows of one index of fsdp go 24 to each index of fsdp; the block of 384 minibatch positions of index j holds at positions j * 384 + s * 24 + c the rows from index s; a permutation of all rows.
All inputs are finite; a program needn't handle non-finite values. No bound on the sum of `done` on one device may be relied on, other than what follows from the above.
Results may differ from the reference program's by a relative error of at most 0.0095.
Values may be sent and summed in bfloat16 or wider, within the bound.
A program may use at most 128 MiB of HBM per device.

```python
import jax
import jax.numpy as jnp
from jax import lax

D = 2048
ACT = 12
STEPS = 24
ENVS = 256
ROWS_DEV = 384
ROWS = 6144
PEER = 24
N_FSDP = 16


def draw_reward(key, part):
    first = jax.random.fold_in(jax.random.fold_in(key, 11), 0)
    env_pos = jnp.arange(ENVS, dtype=jnp.float32) / ENVS
    rising = jnp.exp(jnp.log(3.0) * env_pos)[:, None]
    values = jnp.clip(jax.random.normal(first, (ENVS, STEPS), jnp.float32), -5.0, 5.0) * rising
    return jnp.clip(values, -22.0, 22.0).astype(jnp.float32)


def draw_minibatch_perm(key, part):
    keys = jax.random.split(jax.random.fold_in(key, 23), N_FSDP)
    shuffled = jax.vmap(lambda single: jax.random.permutation(single, ROWS_DEV))(keys).astype(jnp.int32)
    source = jnp.arange(N_FSDP, dtype=jnp.int32)[:, None]
    target = shuffled // PEER
    within = shuffled % PEER
    return (target * ROWS_DEV + source * PEER + within).reshape(-1).astype(jnp.int32)


def place_ends(result, own_key, low, high):
    spot = [jax.random.randint(jax.random.fold_in(own_key, axis), (), 0, length) for axis, length in enumerate(result.shape)]
    longest = result.shape.index(max(result.shape))
    neighbour = spot[:longest] + [(spot[longest] + 1) % result.shape[longest]] + spot[longest + 1:]
    return result.at[tuple(spot)].set(low).at[tuple(neighbour)].set(high)


def level_of(key, shape, cuts, low, top_value):
    def one(dim, parts):
        steps = jax.random.uniform(jax.random.fold_in(jax.random.fold_in(key, 6), dim), (parts,), jnp.float32, low / len(cuts), top_value / len(cuts))
        return jnp.repeat(jnp.exp(steps), shape[dim] // parts).reshape((-1,) + (1,) * (len(shape) - dim - 1))

    loudness = one(*cuts[0])
    for cut in cuts[1:]:
        loudness = loudness * one(*cut)
    return loudness


def gaussian(stream_key, dims, deviation, limit, shards=(), kind=jnp.bfloat16):
    array = jax.random.normal(stream_key, dims, jnp.float32) * deviation
    if len(shards) > 0:
        array = level_of(stream_key, dims, shards, -0.22, 0.18) * array
    return jnp.clip(array, min=-limit, max=limit).astype(kind)


def setup_inputs(seed: int = 0, part: int = 0) -> dict:
    seeds = jax.random.split(jax.random.key(seed), 12)
    own_keys = jax.random.split(jax.random.fold_in(seeds[11], part), 12)
    return {
        "obs_feat": gaussian(own_keys[0], (ROWS, D), 1.0, 6.0, ((0, 16),)),
        "reward": draw_reward(jax.random.fold_in(jax.random.fold_in(seeds[11], part), 71), part),
        "value_old": gaussian(own_keys[2], (ENVS, STEPS + 1), 1.0, 6.0, ((0, 16),), jnp.float32),
        "done": place_ends((jax.random.randint(own_keys[3], (ENVS, STEPS), 0, 32) < 1).astype(jnp.int32), jax.random.fold_in(own_keys[3], 1), 0, 1),
        "minibatch_perm": draw_minibatch_perm(jax.random.fold_in(jax.random.fold_in(seeds[11], part), 71), part),
        "old_mean": gaussian(own_keys[5], (ROWS, ACT), 1.0, 6.0, ((0, 16),)),
        "noise": gaussian(own_keys[6], (ROWS, ACT), 1.0, 6.0, ((0, 16),)),
        "gain_in": jnp.clip(1.0 + 0.1 * jax.random.normal(seeds[7], (D,), jnp.float32), 0.5, 1.5),
        "out_weight": gaussian(seeds[8], (D, D), D ** -0.5, 0.125, ((0, 16),)),
        "head_weight": gaussian(seeds[9], (D, ACT + 1), D ** -0.5, 0.125),
        "log_std": jnp.clip(jax.random.uniform(seeds[10], (ACT,), jnp.float32, 0.7, 1.3), 0.7, 1.3),
    }


GAMMA = 0.99
LAMBDA_GAE = 0.95
CLIP_EPS = 0.2
NORM_EPS = 1e-05

def advantages(reward, value_old, done):
    keep = 1.0 - done.astype(jnp.float32)
    deltas = reward + GAMMA * value_old[:, 1:] * keep - value_old[:, :-1]

    def walk(carry, inputs):
        dstep, kstep = inputs
        carry = dstep + GAMMA * LAMBDA_GAE * kstep * carry
        return (carry, carry)
    start = jnp.zeros((reward.shape[0],), jnp.float32)
    _, stacked = lax.scan(walk, start, (deltas.T, keep.T), reverse=True)
    gae = stacked.T
    return (gae.reshape(-1), (gae + value_old[:, :-1]).reshape(-1))

def row_block(rows_x, old_mean, noise, adv_b, ret_b, gain_in, out_weight, head_weight, log_std, scale):
    xf = rows_x.astype(jnp.float32)
    normed = (xf * lax.rsqrt(lax.optimization_barrier(jnp.mean(xf * xf, -1, keepdims=True)) + NORM_EPS) * gain_in).astype(jnp.bfloat16)
    hidden = xf + jnp.dot(normed, out_weight, preferred_element_type=jnp.float32)
    rinv = lax.rsqrt(lax.optimization_barrier(jnp.mean(hidden * hidden, -1, keepdims=True)) + NORM_EPS)
    hnorm = hidden * rinv
    hnorm_b = hnorm.astype(jnp.bfloat16)
    heads = jnp.dot(hnorm_b, head_weight, preferred_element_type=jnp.float32)
    nact = log_std.shape[0]
    mean_act = heads[:, :nact]
    value = heads[:, nact]
    std_dev = jnp.exp(log_std)
    offset = old_mean.astype(jnp.float32) - mean_act
    sample = noise.astype(jnp.float32)
    logr = lax.optimization_barrier(jnp.sum(-sample * offset / std_dev - offset * offset / (2.0 * std_dev * std_dev), -1))
    ratio = jnp.exp(logr)
    advant = adv_b.astype(jnp.float32)
    clipped = jnp.clip(ratio, 1.0 - CLIP_EPS, 1.0 + CLIP_EPS)
    active = ratio * advant <= clipped * advant
    gratio = jnp.where(active, -scale * advant, 0.0)
    glogr = gratio * ratio
    gmean = glogr[:, None] * (sample / std_dev + offset / (std_dev * std_dev))
    gvalue = scale * (value - ret_b.astype(jnp.float32))
    std_part = lax.optimization_barrier(jnp.sum(glogr[:, None] * (sample * offset / std_dev + offset * offset / (std_dev * std_dev)), 0))
    ghead = jnp.concatenate([gmean, gvalue[:, None]], 1)
    head_part = jnp.dot(hnorm_b.astype(jnp.float32).T, ghead, precision=lax.Precision.HIGHEST)
    ghn = jnp.dot(ghead, head_weight.astype(jnp.float32).T, precision=lax.Precision.HIGHEST)
    ghid = rinv * (ghn - hnorm * lax.optimization_barrier(jnp.mean(ghn * hnorm, -1, keepdims=True)))
    ghid_b = ghid.astype(jnp.bfloat16)
    return (hidden.astype(jnp.bfloat16), normed, ghid_b, head_part, std_part)

def reference(obs_feat, reward, value_old, done, minibatch_perm, old_mean, noise, gain_in, out_weight, head_weight, log_std):
    gae, returns = advantages(reward, value_old, done)
    mean_adv = jnp.sum(gae) / ROWS
    var_adv = jnp.sum(gae * gae) / ROWS - mean_adv * mean_adv
    adv_b = ((gae - mean_adv) * lax.rsqrt(var_adv + NORM_EPS)).astype(jnp.bfloat16)
    ret_b = returns.astype(jnp.bfloat16)
    scale = 1.0 / jnp.sqrt(jnp.float32(ROWS))
    nblock = ROWS // ROWS_DEV

    def one_block(carry, inputs):
        wsum, hsum, ssum = carry
        bx, bm, bn, ba, br = inputs
        hid_b, normed, ghid_b, head_part, std_part = row_block(bx, bm, bn, ba, br, gain_in, out_weight, head_weight, log_std, scale)
        wpart = lax.dot_general(normed, ghid_b, (((0,), (0,)), ((), ())), preferred_element_type=jnp.float32)
        return ((wsum + wpart, hsum + head_part, ssum + std_part), hid_b)
    init = (jnp.zeros((D, D), jnp.float32), jnp.zeros((D, ACT + 1), jnp.float32), jnp.zeros((ACT,), jnp.float32))
    inputs = (obs_feat.reshape(nblock, ROWS_DEV, D), old_mean.reshape(nblock, ROWS_DEV, ACT), noise.reshape(nblock, ROWS_DEV, ACT), adv_b.reshape(nblock, ROWS_DEV), ret_b.reshape(nblock, ROWS_DEV))
    (grad_weight, grad_head, grad_std), hid_all = lax.scan(one_block, init, inputs)
    hidden_out = jnp.zeros((ROWS, D), jnp.bfloat16).at[minibatch_perm].set(hid_all.reshape(ROWS, D))
    return (hidden_out, grad_weight, grad_head, grad_std)
```

```python
import functools

import jax
import jax.numpy as jnp
from jax import lax
from jax.experimental import pallas as pl
from jax.experimental.pallas import tpu as pltpu
from jax.sharding import PartitionSpec as P

GAMMA = 0.99
LAMBDA_GAE = 0.95
CLIP_EPS = 0.2
NORM_EPS = 1e-05
MESH = pl.DeviceIdType.MESH
LANES = 128
F32 = jnp.float32
BF16 = jnp.bfloat16


def chip_at(pos, ring):
    half = ring // 2
    col = pos // half
    row = col * (ring - 1 - pos) + (1 - col) * pos
    return 2 * row + col


class Place:
    def __init__(self, n):
        self.n = n
        self.me = lax.axis_index("fsdp")
        self.group = lax.axis_index("groups")
        self.ring = n // 2
        self.rows = n // 4
        self.core = lax.rem(self.me, 2)
        chip = self.me // 2
        self.col = lax.rem(chip, 2)
        self.row = chip // 2
        self.pos = self.col * (self.ring - 1 - self.row) + (1 - self.col) * self.row
        self.step = 1 - 2 * self.core
        self.sibling = self.me + self.step

    def on_ring(self, ahead, core):
        pos = lax.rem(self.pos + ahead + self.ring, self.ring)
        return 2 * chip_at(pos, self.ring) + core

    def at(self, row, col, core):
        return (row * 2 + col) * 2 + core


def remote(src, dst, send, recv, device):
    return pltpu.make_async_remote_copy(
        src_ref=src, dst_ref=dst, send_sem=send, recv_sem=recv, device_id=device, device_id_type=MESH
    )


def await_bytes(part, sem):
    pltpu.make_async_copy(part, part, sem).wait()


def halves(start, size):
    first = (size // LANES + 1) // 2 * LANES
    return [(start, first), (start + first, size - first)]


def lanes(start, size):
    return pl.ds(pl.multiple_of(start, LANES), size)


def kernel(
    n, steps,
    x_hbm, w_hbm, gain_ref, reward_ref, value_ref, done_ref, perm_ref, mean_ref, noise_ref, head_ref, std_ref,
    hid_ref, grad_ref, headg_ref, stdg_ref,
    xv, held, normed, hidden, hnorm, ghid, place, send, rows_t, cols, envs, head, lstd,
    stats, stat_own, head_blk, head_in, head_sum, head_all,
    sib_out, sib_in, y_out, y_in, z_out, z_in, own, prod,
    load_sems, ring_send, ring_recv, x_send, x_recv, sibr_recv, sibx_recv, sib_send,
    stat_send, stat_recv, a2a_send, a2a_recv, head_sems,
    rs_sib_send, rs_sib_recv, y_send, y_recv, z_send, z_recv,
):
    p = Place(n)
    me, last, L = p.me, p.ring - 1, p.rows
    rows, width = xv.shape
    shard = w_hbm.shape[0]
    block = normed.shape[2]
    whole_blocks = shard == block
    nact = mean_ref.shape[0]
    n_env = reward_ref.shape[0]
    slot_rows = send.shape[1]
    per = rows // n
    tile = width // 4
    tiles = [pl.ds(j * tile, tile) for j in range(4)]
    total_rows = rows * n

    load_x = pltpu.make_async_copy(x_hbm, xv, load_sems.at[0])
    load_x.start()
    load_w = pltpu.make_async_copy(w_hbm, held.at[pl.ds(pl.multiple_of(me * shard, shard), shard)], load_sems.at[1])
    load_w.start()

    barrier = pltpu.get_barrier_semaphore()

    @pl.loop(1, n)
    def _(k):
        pl.semaphore_signal(barrier, inc=1, device_id={"fsdp": lax.rem(me + k, n)}, device_id_type=MESH)

    pl.semaphore_signal(barrier, inc=1, device_id={"groups": 1 - p.group}, device_id_type=MESH)
    pl.semaphore_wait(barrier, n)

    xw = width // LANES * 5 // 16 * LANES
    rest = width - 2 * xw
    ring_cuts = halves(p.group * (width - xw), xw) + halves(xw, rest)
    x_cuts = halves((1 - p.group) * (width - xw), xw)
    next_chip = {"fsdp": p.on_ring(p.step, p.core)}
    sibling = {"fsdp": p.sibling}
    partner = {"groups": 1 - p.group}

    def part(owner, cut):
        return held.at[pl.ds(pl.multiple_of(owner * shard, shard), shard), lanes(*cut)]

    def ring_copy(owner, s, i):
        ref = part(owner, ring_cuts[i])
        return remote(ref, ref, ring_send, ring_recv.at[s, i], next_chip)

    def x_copy(owner, s, i):
        ref = part(owner, ring_cuts[i])
        return remote(ref, ref, x_send, x_recv.at[s, i], partner)

    def x_arrival(owner, s, i):
        ref = part(owner, x_cuts[i])
        return remote(ref, ref, x_send, x_recv.at[s, i], partner)

    def sibr_copy(owner, s, i):
        ref = part(owner, ring_cuts[i])
        return remote(ref, ref, sib_send, sibr_recv.at[s, i], sibling)

    def sibx_copy(owner, s, i):
        ref = part(owner, x_cuts[i])
        return remote(ref, ref, sib_send, sibx_recv.at[s, i], sibling)

    def mine(s):
        return p.on_ring(-p.step * s, p.core)

    def theirs(s):
        return p.on_ring(p.step * s, 1 - p.core)

    load_w.wait()
    for i in range(4):
        ring_copy(me, 1, i).start()
    for i in range(4):
        sibr_copy(me, 0, i).start()
    for i in range(2):
        sibx_copy(me, 0, i).start()

    load_x.wait()
    square = jnp.zeros((rows, LANES), F32)
    for j in range(0, width, LANES):
        xf = xv[:, j : j + LANES].astype(F32)
        square = square + xf * xf
    scale_x = lax.rsqrt(jnp.sum(square, -1, keepdims=True) / width + NORM_EPS)
    for j in range(width // block):
        at = pl.ds(j * block, block)
        xf = xv[:, at].astype(F32)
        hidden[:, at] = xf
        normed[j] = (xf * scale_x * gain_ref[:, at]).astype(BF16)

    def add(index):
        for cut in tiles:
            hidden[:, cut] += jnp.dot(
                normed[index], held[pl.ds(pl.multiple_of(index * block, block), block), cut],
                preferred_element_type=F32,
            )

    def add_shard(owner):
        if whole_blocks:
            add(owner)

    def spread(count, source_of, dst, send_sem, recv_sem):
        @pl.loop(1, n)
        def _(k):
            peer = lax.rem(me + k, n)

            def go():
                remote(source_of(peer), dst.at[me], send_sem, recv_sem, {"fsdp": peer}).start()

            if count == n:
                go()
            else:
                pl.when(peer < count)(go)

    def advantages():
        lane = lax.broadcasted_iota(jnp.int32, (n_env, LANES), 1)
        envs[...] = jnp.zeros_like(envs)
        envs[0, :, 0:steps] = reward_ref[...]
        envs[1, :, 0 : steps + 1] = value_ref[...]
        envs[2, :, 0:steps] = 1.0 - done_ref[...].astype(F32)
        value, keep = envs[1], envs[2]
        ahead = pltpu.roll(value, LANES - 1, 1)
        gae = jnp.where(lane < steps, envs[0] + GAMMA * ahead * keep - value, 0.0)
        decay = GAMMA * LAMBDA_GAE * keep
        shift = 1
        while shift < steps:
            gae = gae + decay * pltpu.roll(gae, LANES - shift, 1)
            decay = decay * pltpu.roll(decay, LANES - shift, 1)
            shift *= 2
        envs[0] = gae
        envs[3] = gae + value
        spot = lax.broadcasted_iota(jnp.int32, (8, LANES), 1)
        stat_own[...] = jnp.where(spot == 0, jnp.sum(gae), jnp.where(spot == 1, jnp.sum(gae * gae), 0.0))
        stats[me] = stat_own[...]
        spread(n, lambda peer: stat_own, stats, stat_send, stat_recv)
        at_step = lax.broadcasted_iota(jnp.int32, (steps, LANES), 0) == lax.broadcasted_iota(
            jnp.int32, (steps, LANES), 1
        )
        for e in range(n_env):
            for c, k in ((0, 0), (1, 3)):
                line = jnp.broadcast_to(envs[k, e : e + 1, :], (steps, LANES))
                cols[c, e * steps : (e + 1) * steps, :] = jnp.broadcast_to(
                    jnp.sum(jnp.where(at_step, line, 0.0), -1, keepdims=True), (steps, LANES)
                )

    def placement():
        perm = perm_ref[...]
        to = lax.div(perm, rows)
        slot = to * slot_rows + lax.rem(perm, per)
        place[...] = jnp.where(
            lax.broadcasted_iota(jnp.int32, place.shape, 0) == slot, 1.0, 0.0
        ).astype(BF16)

    def columns():
        for k, ref in ((0, mean_ref), (1, noise_ref)):
            rows_t[...] = jnp.zeros_like(rows_t)
            rows_t[0:nact] = ref[...].astype(F32)
            rows_t[16 : 16 + nact] = ref[...].astype(F32)
            cols[2 + k] = jnp.transpose(rows_t[...])
        head[...] = jnp.zeros_like(head)
        hf = head_ref[...].astype(F32)
        head[0 : nact + 1] = hf
        head[16 : 17 + nact] = hf
        lstd[...] = jnp.zeros_like(lstd)
        lstd[0:1, 0:nact] = std_ref[...]
        lstd[0:1, 16 : 16 + nact] = std_ref[...]

    def hop(s, _):
        owner = mine(s)
        for i in range(4):
            ring_copy(owner, s, i).wait_recv()

            @pl.when(s < last)
            def _():
                ring_copy(owner, s + 1, i).start()

            if i < 2:
                x_copy(owner, s, i).start()
            sibr_copy(owner, s, i).start()
        before = mine(s - 1)

        @pl.when(s > 1)
        def _():
            for i in range(2):
                x_arrival(before, s - 1, i).wait_recv()
                sibx_copy(before, s - 1, i).start()

        add_shard(before)

        @pl.when(s == 1)
        def _():
            advantages()

        @pl.when(s == 2)
        def _():
            placement()

        @pl.when(s == 3)
        def _():
            columns()

        @pl.when(s > 1)
        def _():
            other = theirs(s - 2)
            for i in range(4):
                sibr_copy(other, s - 2, i).wait_recv()
            for i in range(2):
                sibx_copy(other, s - 2, i).wait_recv()
            add_shard(other)

        return 0

    lax.fori_loop(1, p.ring, hop, 0)
    for i in range(2):
        x_arrival(mine(last), last, i).wait_recv()
        sibx_copy(mine(last), last, i).start()
    for s in (last - 1, last):
        other = theirs(s)
        if s == last:
            add_shard(mine(last))
        for i in range(4):
            sibr_copy(other, s, i).wait_recv()
        for i in range(2):
            sibx_copy(other, s, i).wait_recv()
        if s < last:
            add_shard(other)
    if not whole_blocks:
        lax.fori_loop(0, width // block - 1, lambda b, _: (add(b), 0)[1], 0)
    final = theirs(last) if whole_blocks else width // block - 1

    square = jnp.zeros((rows, LANES), F32)
    for cut in tiles:
        h = hidden[:, cut] + jnp.dot(
            normed[final], held[pl.ds(pl.multiple_of(final * block, block), block), cut],
            preferred_element_type=F32,
        )
        hidden[:, cut] = h
        for j in range(0, tile, LANES):
            piece = h[:, j : j + LANES]
            square = square + piece * piece
        moved = jnp.dot(place[...], h.astype(BF16), preferred_element_type=F32).astype(BF16)
        send[:, :, cut] = moved.reshape(n, slot_rows, tile)

    def row_copy(peer):
        return remote(send.at[peer], hid_ref.at[me], a2a_send, a2a_recv, {"fsdp": peer})

    def same_line():
        row_copy(p.sibling).start()

        @pl.loop(1, L)
        def _(k):
            to = lax.rem(p.row + k, L)
            row_copy(p.at(to, p.col, 0)).start()
            row_copy(p.at(to, p.col, 1)).start()

    def other_line(m):
        to = lax.rem(p.row + L // 2 + m, L)
        row_copy(p.at(to, 1 - p.col, 0)).start()
        row_copy(p.at(to, 1 - p.col, 1)).start()

    other_line(0)
    same_line()
    stay = pltpu.make_async_copy(send.at[me], hid_ref.at[me], load_sems.at[2])
    stay.start()

    rinv = lax.rsqrt(jnp.sum(square, -1, keepdims=True) / width + NORM_EPS)
    headb = head[...].astype(BF16)
    heads = jnp.zeros((rows, LANES), F32)
    for j, cut in enumerate(tiles):
        hb = (hidden[:, cut] * rinv).astype(BF16)
        hnorm[:, cut] = hb
        heads = heads + lax.dot_general(
            hb, headb[:, j * tile : (j + 1) * tile], (((1,), (1,)), ((), ())), preferred_element_type=F32
        )
    await_bytes(stats.at[pl.ds(0, n - 1)], stat_recv)
    sums = jnp.sum(stats[...], 0)
    mean_adv = sums[0:1, 0:1] / total_rows
    var_adv = sums[0:1, 1:2] / total_rows - mean_adv * mean_adv
    advant = ((cols[0, :, 0:1] - mean_adv) * lax.rsqrt(var_adv + NORM_EPS)).astype(BF16).astype(F32)
    ret = cols[1, :, 0:1].astype(BF16).astype(F32)
    lane = lax.broadcasted_iota(jnp.int32, (1, LANES), 1)
    one = lax.rem(lane, 16)
    first = lane < 16
    is_act = (one < nact) & (lane < 32)
    is_value = (one == nact) & (lane < 32)
    inv = jnp.where(is_act, jnp.exp(-lstd[0:1, :]), 0.0)
    noise = cols[3]
    u = (cols[2] - heads) * inv
    logr = jnp.sum(jnp.where(first, -noise * u - 0.5 * u * u, 0.0), -1, keepdims=True)
    ratio = jnp.exp(logr)
    scale = 1.0 / jnp.sqrt(jnp.full((1, 1), total_rows, F32))
    clipped = jnp.clip(ratio, 1.0 - CLIP_EPS, 1.0 + CLIP_EPS)
    active = ratio * advant <= clipped * advant
    glogr = jnp.where(active, -scale * advant, 0.0) * ratio
    ghead = jnp.where(is_value, scale * (heads - ret), glogr * (inv * (noise + u)))
    std_part = jnp.sum(glogr * (noise * u + u * u), 0, keepdims=True)
    along = jnp.sum(jnp.where(first, ghead * heads, 0.0), -1, keepdims=True) / width
    pull = rinv * rinv * along

    def two_parts(value):
        high = value.astype(BF16)
        return jnp.where(first, high.astype(F32), value - high.astype(F32)).astype(BF16)

    gscaled = two_parts(ghead * rinv)
    for j, cut in enumerate(tiles):
        g = jnp.dot(gscaled, headb[:, j * tile : (j + 1) * tile], preferred_element_type=F32)
        ghid[:, cut] = (g - hidden[:, cut] * pull).astype(BF16)

    def product(owner, cut):
        index = owner if whole_blocks else owner * shard // block
        value = lax.dot_general(
            normed[index], ghid[:, cut], (((0,), (0,)), ((), ())), preferred_element_type=F32
        )
        if whole_blocks:
            return value
        prod[...] = value
        return prod[pl.ds(pl.multiple_of(lax.rem(owner * shard, block), shard), shard)]

    def target(k):
        up = k < L - 1 - p.row
        return jnp.where(up, L - 1 - k, jnp.where(k < L - 1, k - (L - 1 - p.row), p.row))

    def sib_copy(slot, j):
        return remote(
            sib_out.at[slot, :, tiles[j]], sib_in.at[slot, :, tiles[j]], rs_sib_send, rs_sib_recv.at[slot, j], sibling
        )

    def y_copy(k, j):
        return remote(
            y_out.at[k, :, tiles[j]], y_in.at[k, :, tiles[j]], y_send, y_recv.at[k, j],
            {"fsdp": p.at(p.row, 1 - p.col, p.core)},
        )

    def for_sibling(k, cross):
        slot = 2 * k + cross
        owner = p.at(target(k), (1 - p.col) if cross else p.col, 1 - p.core)
        for j, cut in enumerate(tiles):
            sib_out[slot, :, cut] = product(owner, cut).astype(BF16)
            sib_copy(slot, j).start()

    def for_me(k, cross):
        owner = p.at(target(k), (1 - p.col) if cross else p.col, p.core)
        for cut in tiles:
            own[:, cut] = product(owner, cut)

    def send_y(k):
        for_sibling(k, 1)
        for_me(k, 1)
        for j, cut in enumerate(tiles):
            sib_copy(2 * k + 1, j).wait_recv()
            y_out[k, :, cut] = (own[:, cut] + sib_in[2 * k + 1, :, cut].astype(F32)).astype(BF16)
            y_copy(k, j).start()

    def chip_sum(k, j):
        cut = tiles[j]
        sib_copy(2 * k, j).wait_recv()
        y_copy(k, j).wait_recv()
        return own[:, cut] + sib_in[2 * k, :, cut].astype(F32) + y_in[k, :, cut].astype(F32)

    def z_copy(to, slot, t, j, row):
        return remote(
            z_out.at[t, :, tiles[j]], z_in.at[slot, :, tiles[j]], z_send, z_recv.at[slot, j],
            {"fsdp": p.at(row, p.col, p.core)},
        )

    def z_arrival(slot, j):
        return remote(
            z_out.at[0, :, tiles[j]], z_in.at[slot, :, tiles[j]], z_send, z_recv.at[slot, j],
            {"fsdp": p.sibling},
        )

    send_y(0)

    gparts = two_parts(ghead)
    row = lax.broadcasted_iota(jnp.int32, (16, LANES), 0)
    for j, cut in enumerate(tiles):
        part_sum = lax.dot_general(gparts, hnorm[:, cut], (((0,), (0,)), ((), ())), preferred_element_type=F32)
        both = part_sum[0:16] + part_sum[16:32]
        for i in range(tile // LANES):
            head_blk[j * (tile // LANES) + i] = jnp.where(
                row == nact + 1, std_part, both[:, i * LANES : (i + 1) * LANES]
            )
    nb = head_all.shape[0]
    is_reducer = me < nb

    def when_reducer(go):
        if nb == n:
            go()
        else:
            pl.when(is_reducer)(go)

    def keep_block():
        head_in[me] = head_blk[me]

    when_reducer(keep_block)
    spread(nb, lambda peer: head_blk.at[peer], head_in, head_sems.at[0], head_sems.at[1])

    def reduce_heads():
        def go():
            await_bytes(head_in.at[pl.ds(0, n - 1)], head_sems.at[1])
            head_sum[...] = jnp.sum(head_in[...], 0)
            head_all[me] = head_sum[...]
            spread(n, lambda peer: head_sum, head_all, head_sems.at[2], head_sems.at[3])

        when_reducer(go)

    def stage(k, _):
        other_line(k + 1)
        send_y(k + 1)
        for_sibling(k, 0)
        for_me(k, 0)
        t = target(k)
        up = k < L - 1 - p.row
        has_in = jnp.where(up, p.row > 0, p.row < L - 1)
        to = jnp.where(up, p.row + 1, p.row - 1)
        slot = jnp.where((t == to) & jnp.logical_not(up), L, t)
        for j, cut in enumerate(tiles):
            total = chip_sum(k, j)
            own[:, cut] = total

            @pl.when(has_in)
            def _():
                z_arrival(t, j).wait_recv()
                own[:, cut] += z_in[t, :, cut].astype(F32)

            z_out[t, :, cut] = own[:, cut].astype(BF16)
            z_copy(to, slot, t, j, to).start()

        @pl.when(k == 1)
        def _():
            reduce_heads()

        return 0

    lax.fori_loop(0, L - 1, stage, 0)
    for_sibling(L - 1, 0)
    for_me(L - 1, 0)
    for j, cut in enumerate(tiles):
        grad_ref[:, cut] = chip_sum(L - 1, j)

        @pl.when(p.row > 0)
        def _():
            z_arrival(p.row, j).wait_recv()
            grad_ref[:, cut] += z_in[p.row, :, cut].astype(F32)

        @pl.when(p.row < L - 1)
        def _():
            z_arrival(L, j).wait_recv()
            grad_ref[:, cut] += z_in[L, :, cut].astype(F32)

    if nb == n:
        await_bytes(head_all.at[pl.ds(0, nb - 1)], head_sems.at[3])
    else:
        @pl.when(is_reducer)
        def _():
            await_bytes(head_all.at[pl.ds(0, nb - 1)], head_sems.at[3])

        @pl.when(jnp.logical_not(is_reducer))
        def _():
            await_bytes(head_all.at[pl.ds(0, nb)], head_sems.at[3])

    for j in range(nb):
        headg_ref[:, j * LANES : (j + 1) * LANES] = head_all[j, 0 : nact + 1, :]
    stdg_ref[...] = head_all[0, nact + 1 : nact + 2, 0:nact]
    await_bytes(hid_ref.at[pl.ds(0, n - 1)], a2a_recv)
    stay.wait()
    await_bytes(send.at[pl.ds(0, n - 1)], a2a_send)
    await_bytes(held.at[pl.ds(0, last * shard), pl.ds(0, width - xw)], ring_send)
    await_bytes(held.at[pl.ds(0, last * shard), pl.ds(0, xw)], x_send)
    await_bytes(held.at[pl.ds(0, p.ring * shard)], sib_send)
    await_bytes(stats.at[pl.ds(0, n - 1)], stat_send)
    if nb == n:
        await_bytes(head_blk.at[pl.ds(0, nb - 1)], head_sems.at[0])
        await_bytes(head_in.at[pl.ds(0, n - 1)], head_sems.at[2])
    else:
        @pl.when(is_reducer)
        def _():
            await_bytes(head_blk.at[pl.ds(0, nb - 1)], head_sems.at[0])
            await_bytes(head_in.at[pl.ds(0, n - 1)], head_sems.at[2])

        @pl.when(jnp.logical_not(is_reducer))
        def _():
            await_bytes(head_blk.at[pl.ds(0, nb)], head_sems.at[0])

    await_bytes(sib_out, rs_sib_send)
    await_bytes(y_out, y_send)
    await_bytes(z_out.at[pl.ds(0, L - 1)], z_send)


def local(
    obs_feat, reward, value_old, done, minibatch_perm, old_mean, noise, gain_in, out_weight, head_weight, log_std
):
    rows, width = obs_feat.shape
    n = lax.axis_size("fsdp")
    steps = reward.shape[1]
    n_env = reward.shape[0]
    nact = log_std.shape[0]
    shard = out_weight.shape[0]
    block = max(shard, LANES)
    per = rows // n
    slot_rows = -(-per // 8) * 8
    L = n // 4
    ring = n // 2
    nb = min(n, width // LANES)
    vmem = pl.BlockSpec(memory_space=pltpu.VMEM)
    hbm = pl.BlockSpec(memory_space=pl.ANY)
    sem = pltpu.SemaphoreType.DMA
    V = pltpu.VMEM
    hid, grad, headg, stdg = pl.pallas_call(
        functools.partial(kernel, n, steps),
        name="step",
        out_shape=(
            jax.ShapeDtypeStruct((n, slot_rows, width), BF16),
            jax.ShapeDtypeStruct((shard, width), F32),
            jax.ShapeDtypeStruct((nact + 1, width), F32),
            jax.ShapeDtypeStruct((1, nact), F32),
        ),
        in_specs=[hbm, hbm] + [vmem] * 9,
        out_specs=(hbm, vmem, vmem, vmem),
        scratch_shapes=[
            V((rows, width), BF16),
            V((width, width), BF16),
            V((width // block, rows, block), BF16),
            V((rows, width), F32),
            V((rows, width), BF16),
            V((rows, width), BF16),
            V((n * slot_rows, rows), BF16),
            V((n, slot_rows, width), BF16),
            V((LANES, rows), F32),
            V((4, rows, LANES), F32),
            V((4, n_env, LANES), F32),
            V((LANES, width), F32),
            V((8, LANES), F32),
            V((n, 8, LANES), F32),
            V((8, LANES), F32),
            V((nb, 16, LANES), F32),
            V((n, 16, LANES), F32),
            V((16, LANES), F32),
            V((nb, 16, LANES), F32),
            V((2 * L, shard, width), BF16),
            V((2 * L, shard, width), BF16),
            V((L, shard, width), BF16),
            V((L, shard, width), BF16),
            V((L, shard, width), BF16),
            V((L + 1, shard, width), BF16),
            V((shard, width), F32),
            V((block, width // 4), F32),
            sem((3,)),
            sem(()),
            sem((ring, 4)),
            sem(()),
            sem((ring, 2)),
            sem((ring, 4)),
            sem((ring, 2)),
            sem(()),
            sem(()),
            sem(()),
            sem(()),
            sem(()),
            sem((4,)),
            sem(()),
            sem((2 * L, 4)),
            sem(()),
            sem((L, 4)),
            sem(()),
            sem((L + 1, 4)),
        ],
        compiler_params=pltpu.CompilerParams(
            collective_id=0, has_side_effects=True, vmem_limit_bytes=60 << 20
        ),
        cost_estimate=pl.CostEstimate(
            flops=4 * rows * width * width, bytes_accessed=16 * rows * width, transcendentals=0
        ),
    )(
        obs_feat, out_weight, gain_in[None, :], reward, value_old, done, minibatch_perm[None, :],
        old_mean.T, noise.T, head_weight.T, log_std[None, :],
    )
    hid = hid[:, :per].reshape(rows, width)
    return (hid, grad, headg.T, stdg[0])


def solution(mesh):
    both = P(("groups", "fsdp"), None)
    return jax.shard_map(
        local,
        mesh=mesh,
        in_specs=(
            both, both, both, both, P(("groups", "fsdp")), both, both, P(), P("fsdp", None), P(), P(),
        ),
        out_specs=(both, both, P("groups", None), P("groups")),
        check_vma=False,
    )
```

```python
import functools

import jax
import jax.numpy as jnp
from jax import lax
from jax.experimental import pallas as pl
from jax.experimental.pallas import tpu as pltpu
from jax.sharding import PartitionSpec as P

GAMMA = 0.99
LAMBDA_GAE = 0.95
CLIP_EPS = 0.2
NORM_EPS = 1e-05
MESH = pl.DeviceIdType.MESH
LANES = 128
F32 = jnp.float32
BF16 = jnp.bfloat16


def chip_at(pos, ring):
    half = ring // 2
    col = pos // half
    row = col * (ring - 1 - pos) + (1 - col) * pos
    return 2 * row + col


class Place:
    def __init__(self, n):
        self.n = n
        self.me = lax.axis_index("fsdp")
        self.group = lax.axis_index("groups")
        self.ring = n // 2
        self.rows = n // 4
        self.core = lax.rem(self.me, 2)
        chip = self.me // 2
        self.col = lax.rem(chip, 2)
        self.row = chip // 2
        self.pos = self.col * (self.ring - 1 - self.row) + (1 - self.col) * self.row
        self.step = 1 - 2 * self.core
        self.sibling = self.me + self.step

    def on_ring(self, ahead, core):
        pos = lax.rem(self.pos + ahead + self.ring, self.ring)
        return 2 * chip_at(pos, self.ring) + core

    def at(self, row, col, core):
        return (row * 2 + col) * 2 + core


def remote(src, dst, send, recv, device):
    return pltpu.make_async_remote_copy(
        src_ref=src, dst_ref=dst, send_sem=send, recv_sem=recv, device_id=device, device_id_type=MESH
    )


def await_bytes(part, sem):
    pltpu.make_async_copy(part, part, sem).wait()


def halves(start, size):
    first = (size // LANES + 1) // 2 * LANES
    return [(start, first), (start + first, size - first)]


def lanes(start, size):
    return pl.ds(pl.multiple_of(start, LANES), size)


def kernel(
    n, steps,
    x_hbm, w_hbm, gain_ref, reward_ref, value_ref, done_ref, perm_ref, mean_ref, noise_ref, head_ref, std_ref,
    hid_ref, grad_ref, headg_ref, stdg_ref,
    xv, held, normed, hidden, hnorm, ghid, place, send, rows_t, cols, envs, head, lstd,
    stats, stat_own, head_blk, head_in, head_sum, head_all,
    sib_out, sib_in, y_out, y_in, z_out, z_in, own, prod,
    load_sems, ring_send, ring_recv, x_send, x_recv, sibr_recv, sibx_recv, sib_send,
    stat_send, stat_recv, a2a_send, a2a_recv, head_sems,
    rs_sib_send, rs_sib_recv, y_send, y_recv, z_send, z_recv,
):
    p = Place(n)
    me, last, L = p.me, p.ring - 1, p.rows
    rows, width = xv.shape
    shard = w_hbm.shape[0]
    block = normed.shape[2]
    whole_blocks = shard == block
    nact = mean_ref.shape[0]
    n_env = reward_ref.shape[0]
    slot_rows = send.shape[1]
    per = rows // n
    tile = width // 4
    tiles = [pl.ds(j * tile, tile) for j in range(4)]
    total_rows = rows * n

    load_x = pltpu.make_async_copy(x_hbm, xv, load_sems.at[0])
    load_x.start()
    load_w = pltpu.make_async_copy(w_hbm, held.at[pl.ds(pl.multiple_of(me * shard, shard), shard)], load_sems.at[1])
    load_w.start()

    barrier = pltpu.get_barrier_semaphore()

    @pl.loop(1, n)
    def _(k):
        pl.semaphore_signal(barrier, inc=1, device_id={"fsdp": lax.rem(me + k, n)}, device_id_type=MESH)

    pl.semaphore_signal(barrier, inc=1, device_id={"groups": 1 - p.group}, device_id_type=MESH)
    pl.semaphore_wait(barrier, n)

    xw = width // LANES * 5 // 16 * LANES
    rest = width - 2 * xw
    ring_cuts = halves(p.group * (width - xw), xw) + halves(xw, rest)
    x_cuts = halves((1 - p.group) * (width - xw), xw)
    next_chip = {"fsdp": p.on_ring(p.step, p.core)}
    sibling = {"fsdp": p.sibling}
    partner = {"groups": 1 - p.group}

    def part(owner, cut):
        return held.at[pl.ds(pl.multiple_of(owner * shard, shard), shard), lanes(*cut)]

    def ring_copy(owner, s, i):
        ref = part(owner, ring_cuts[i])
        return remote(ref, ref, ring_send, ring_recv.at[s, i], next_chip)

    def x_copy(owner, s, i):
        ref = part(owner, ring_cuts[i])
        return remote(ref, ref, x_send, x_recv.at[s, i], partner)

    def x_arrival(owner, s, i):
        ref = part(owner, x_cuts[i])
        return remote(ref, ref, x_send, x_recv.at[s, i], partner)

    def sibr_copy(owner, s, i):
        ref = part(owner, ring_cuts[i])
        return remote(ref, ref, sib_send, sibr_recv.at[s, i], sibling)

    def sibx_copy(owner, s, i):
        ref = part(owner, x_cuts[i])
        return remote(ref, ref, sib_send, sibx_recv.at[s, i], sibling)

    def mine(s):
        return p.on_ring(-p.step * s, p.core)

    def theirs(s):
        return p.on_ring(p.step * s, 1 - p.core)

    load_w.wait()
    for i in range(4):
        ring_copy(me, 1, i).start()
    for i in range(4):
        sibr_copy(me, 0, i).start()
    for i in range(2):
        sibx_copy(me, 0, i).start()

    load_x.wait()
    square = jnp.zeros((rows, LANES), F32)
    for j in range(0, width, LANES):
        xf = xv[:, j : j + LANES].astype(F32)
        square = square + xf * xf
    scale_x = lax.rsqrt(jnp.sum(square, -1, keepdims=True) / width + NORM_EPS)
    for j in range(width // block):
        at = pl.ds(j * block, block)
        xf = xv[:, at].astype(F32)
        hidden[:, at] = xf
        normed[j] = (xf * scale_x * gain_ref[:, at]).astype(BF16)

    def add(index):
        for cut in tiles:
            hidden[:, cut] += jnp.dot(
                normed[index], held[pl.ds(pl.multiple_of(index * block, block), block), cut],
                preferred_element_type=F32,
            )

    def add_shard(owner):
        if whole_blocks:
            add(owner)

    def spread(count, source_of, dst, send_sem, recv_sem):
        @pl.loop(1, n)
        def _(k):
            peer = lax.rem(me + k, n)

            def go():
                remote(source_of(peer), dst.at[me], send_sem, recv_sem, {"fsdp": peer}).start()

            if count == n:
                go()
            else:
                pl.when(peer < count)(go)

    def advantages():
        lane = lax.broadcasted_iota(jnp.int32, (n_env, LANES), 1)
        envs[...] = jnp.zeros_like(envs)
        envs[0, :, 0:steps] = reward_ref[...]
        envs[1, :, 0 : steps + 1] = value_ref[...]
        envs[2, :, 0:steps] = 1.0 - done_ref[...].astype(F32)
        value, keep = envs[1], envs[2]
        ahead = pltpu.roll(value, LANES - 1, 1)
        gae = jnp.where(lane < steps, envs[0] + GAMMA * ahead * keep - value, 0.0)
        decay = GAMMA * LAMBDA_GAE * keep
        shift = 1
        while shift < steps:
            gae = gae + decay * pltpu.roll(gae, LANES - shift, 1)
            decay = decay * pltpu.roll(decay, LANES - shift, 1)
            shift *= 2
        envs[0] = gae
        envs[3] = gae + value
        spot = lax.broadcasted_iota(jnp.int32, (8, LANES), 1)
        stat_own[...] = jnp.where(spot == 0, jnp.sum(gae), jnp.where(spot == 1, jnp.sum(gae * gae), 0.0))
        stats[me] = stat_own[...]
        spread(n, lambda peer: stat_own, stats, stat_send, stat_recv)
        at_step = lax.broadcasted_iota(jnp.int32, (steps, LANES), 0) == lax.broadcasted_iota(
            jnp.int32, (steps, LANES), 1
        )
        for e in range(n_env):
            for c, k in ((0, 0), (1, 3)):
                line = jnp.broadcast_to(envs[k, e : e + 1, :], (steps, LANES))
                cols[c, e * steps : (e + 1) * steps, :] = jnp.broadcast_to(
                    jnp.sum(jnp.where(at_step, line, 0.0), -1, keepdims=True), (steps, LANES)
                )

    def placement():
        perm = perm_ref[...].reshape(1, rows)
        to = lax.div(perm, rows)
        slot = to * slot_rows + lax.rem(perm, per)
        place[...] = jnp.where(
            lax.broadcasted_iota(jnp.int32, place.shape, 0) == slot, 1.0, 0.0
        ).astype(BF16)

    def columns():
        for k, ref in ((0, mean_ref), (1, noise_ref)):
            rows_t[...] = jnp.zeros_like(rows_t)
            rows_t[0:nact] = ref[...].astype(F32)
            rows_t[16 : 16 + nact] = ref[...].astype(F32)
            cols[2 + k] = jnp.transpose(rows_t[...])
        head[...] = jnp.zeros_like(head)
        hf = head_ref[...].astype(F32)
        head[0 : nact + 1] = hf
        head[16 : 17 + nact] = hf
        lstd[...] = jnp.zeros_like(lstd)
        lstd[0:1, 0:nact] = std_ref[...]
        lstd[0:1, 16 : 16 + nact] = std_ref[...]

    def hop(s, _):
        owner = mine(s)
        for i in range(4):
            ring_copy(owner, s, i).wait_recv()

            @pl.when(s < last)
            def _():
                ring_copy(owner, s + 1, i).start()

            if i < 2:
                x_copy(owner, s, i).start()
            sibr_copy(owner, s, i).start()
        before = mine(s - 1)

        @pl.when(s > 1)
        def _():
            for i in range(2):
                x_arrival(before, s - 1, i).wait_recv()
                sibx_copy(before, s - 1, i).start()

        add_shard(before)

        @pl.when(s == 1)
        def _():
            advantages()

        @pl.when(s == 2)
        def _():
            placement()

        @pl.when(s == 3)
        def _():
            columns()

        @pl.when(s > 1)
        def _():
            other = theirs(s - 2)
            for i in range(4):
                sibr_copy(other, s - 2, i).wait_recv()
            for i in range(2):
                sibx_copy(other, s - 2, i).wait_recv()
            add_shard(other)

        return 0

    lax.fori_loop(1, p.ring, hop, 0)
    for i in range(2):
        x_arrival(mine(last), last, i).wait_recv()
        sibx_copy(mine(last), last, i).start()
    for s in (last - 1, last):
        other = theirs(s)
        if s == last:
            add_shard(mine(last))
        for i in range(4):
            sibr_copy(other, s, i).wait_recv()
        for i in range(2):
            sibx_copy(other, s, i).wait_recv()
        if s < last:
            add_shard(other)
    if not whole_blocks:
        lax.fori_loop(0, width // block - 1, lambda b, _: (add(b), 0)[1], 0)
    final = theirs(last) if whole_blocks else width // block - 1

    square = jnp.zeros((rows, LANES), F32)
    for cut in tiles:
        h = hidden[:, cut] + jnp.dot(
            normed[final], held[pl.ds(pl.multiple_of(final * block, block), block), cut],
            preferred_element_type=F32,
        )
        hidden[:, cut] = h
        for j in range(0, tile, LANES):
            piece = h[:, j : j + LANES]
            square = square + piece * piece
        moved = jnp.dot(place[...], h.astype(BF16), preferred_element_type=F32).astype(BF16)
        send[:, :, cut] = moved.reshape(n, slot_rows, tile)

    def row_copy(peer):
        return remote(send.at[peer], hid_ref.at[me], a2a_send, a2a_recv, {"fsdp": peer})

    def same_line():
        row_copy(p.sibling).start()

        @pl.loop(1, L)
        def _(k):
            to = lax.rem(p.row + k, L)
            row_copy(p.at(to, p.col, 0)).start()
            row_copy(p.at(to, p.col, 1)).start()

    def other_line(m):
        to = lax.rem(p.row + L // 2 + m, L)
        row_copy(p.at(to, 1 - p.col, 0)).start()
        row_copy(p.at(to, 1 - p.col, 1)).start()

    other_line(0)
    same_line()
    stay = pltpu.make_async_copy(send.at[me], hid_ref.at[me], load_sems.at[2])
    stay.start()

    rinv = lax.rsqrt(jnp.sum(square, -1, keepdims=True) / width + NORM_EPS)
    headb = head[...].astype(BF16)
    heads = jnp.zeros((rows, LANES), F32)
    for j, cut in enumerate(tiles):
        hb = (hidden[:, cut] * rinv).astype(BF16)
        hnorm[:, cut] = hb
        heads = heads + lax.dot_general(
            hb, headb[:, j * tile : (j + 1) * tile], (((1,), (1,)), ((), ())), preferred_element_type=F32
        )
    await_bytes(stats.at[pl.ds(0, n - 1)], stat_recv)
    sums = jnp.sum(stats[...], 0)
    mean_adv = sums[0:1, 0:1] / total_rows
    var_adv = sums[0:1, 1:2] / total_rows - mean_adv * mean_adv
    advant = ((cols[0, :, 0:1] - mean_adv) * lax.rsqrt(var_adv + NORM_EPS)).astype(BF16).astype(F32)
    ret = cols[1, :, 0:1].astype(BF16).astype(F32)
    lane = lax.broadcasted_iota(jnp.int32, (1, LANES), 1)
    one = lax.rem(lane, 16)
    first = lane < 16
    is_act = (one < nact) & (lane < 32)
    is_value = (one == nact) & (lane < 32)
    inv = jnp.where(is_act, jnp.exp(-lstd[0:1, :]), 0.0)
    noise = cols[3]
    u = (cols[2] - heads) * inv
    logr = jnp.sum(jnp.where(first, -noise * u - 0.5 * u * u, 0.0), -1, keepdims=True)
    ratio = jnp.exp(logr)
    scale = 1.0 / jnp.sqrt(jnp.full((1, 1), total_rows, F32))
    clipped = jnp.clip(ratio, 1.0 - CLIP_EPS, 1.0 + CLIP_EPS)
    active = ratio * advant <= clipped * advant
    glogr = jnp.where(active, -scale * advant, 0.0) * ratio
    ghead = jnp.where(is_value, scale * (heads - ret), glogr * (inv * (noise + u)))
    std_part = jnp.sum(glogr * (noise * u + u * u), 0, keepdims=True)
    along = jnp.sum(jnp.where(first, ghead * heads, 0.0), -1, keepdims=True) / width
    pull = rinv * rinv * along

    def two_parts(value):
        high = value.astype(BF16)
        return jnp.where(first, high.astype(F32), value - high.astype(F32)).astype(BF16)

    gscaled = two_parts(ghead * rinv)
    for j, cut in enumerate(tiles):
        g = jnp.dot(gscaled, headb[:, j * tile : (j + 1) * tile], preferred_element_type=F32)
        ghid[:, cut] = (g - hidden[:, cut] * pull).astype(BF16)

    def product(owner, cut):
        index = owner if whole_blocks else owner * shard // block
        value = lax.dot_general(
            normed[index], ghid[:, cut], (((0,), (0,)), ((), ())), preferred_element_type=F32
        )
        if whole_blocks:
            return value
        prod[...] = value
        return prod[pl.ds(pl.multiple_of(lax.rem(owner * shard, block), shard), shard)]

    def goes_up(k):
        up_first = 2 * p.row < L
        return jnp.where(up_first, k < L - 1 - p.row, (k >= p.row) & (k < L - 1))

    def target(k):
        ups, downs = L - 1 - p.row, p.row
        up_first = 2 * p.row < L
        up_at = jnp.where(up_first, k, k - downs)
        down_at = jnp.where(up_first, k - ups, k)
        up = goes_up(k)
        return jnp.where(up, L - 1 - up_at, jnp.where(k < L - 1, down_at, p.row))

    def sib_copy(slot, j):
        return remote(
            sib_out.at[slot, :, tiles[j]], sib_in.at[slot, :, tiles[j]], rs_sib_send, rs_sib_recv.at[slot, j], sibling
        )

    def y_copy(k, j):
        return remote(
            y_out.at[k, :, tiles[j]], y_in.at[k, :, tiles[j]], y_send, y_recv.at[k, j],
            {"fsdp": p.at(p.row, 1 - p.col, p.core)},
        )

    def for_sibling(k, cross):
        slot = 2 * k + cross
        owner = p.at(target(k), (1 - p.col) if cross else p.col, 1 - p.core)
        for j, cut in enumerate(tiles):
            sib_out[slot, :, cut] = product(owner, cut).astype(BF16)
            sib_copy(slot, j).start()

    def for_me(k, cross):
        owner = p.at(target(k), (1 - p.col) if cross else p.col, p.core)
        for cut in tiles:
            own[k, :, cut] = product(owner, cut)

    def send_y(k):
        for_sibling(k, 1)
        for_me(k, 1)
        for j, cut in enumerate(tiles):
            sib_copy(2 * k + 1, j).wait_recv()
            y_out[k, :, cut] = (own[k, :, cut] + sib_in[2 * k + 1, :, cut].astype(F32)).astype(BF16)
            y_copy(k, j).start()

    def chip_sum(k, j):
        cut = tiles[j]
        sib_copy(2 * k, j).wait_recv()
        y_copy(k, j).wait_recv()
        return own[k, :, cut] + sib_in[2 * k, :, cut].astype(F32) + y_in[k, :, cut].astype(F32)

    def z_copy(to, slot, k, j):
        return remote(
            z_out.at[k, :, tiles[j]], z_in.at[slot, :, tiles[j]], z_send, z_recv.at[slot, j],
            {"fsdp": p.at(to, p.col, p.core)},
        )

    def z_arrival(slot, j):
        return remote(
            z_out.at[0, :, tiles[j]], z_in.at[slot, :, tiles[j]], z_send, z_recv.at[slot, j],
            {"fsdp": p.sibling},
        )

    send_y(0)

    gparts = two_parts(ghead)
    row = lax.broadcasted_iota(jnp.int32, (16, LANES), 0)
    for j, cut in enumerate(tiles):
        part_sum = lax.dot_general(gparts, hnorm[:, cut], (((0,), (0,)), ((), ())), preferred_element_type=F32)
        both = part_sum[0:16] + part_sum[16:32]
        for i in range(tile // LANES):
            head_blk[j * (tile // LANES) + i] = jnp.where(
                row == nact + 1, std_part, both[:, i * LANES : (i + 1) * LANES]
            )
    nb = head_all.shape[0]
    is_reducer = me < nb

    def when_reducer(go):
        if nb == n:
            go()
        else:
            pl.when(is_reducer)(go)

    def keep_block():
        head_in[me] = head_blk[me]

    when_reducer(keep_block)
    spread(nb, lambda peer: head_blk.at[peer], head_in, head_sems.at[0], head_sems.at[1])

    def reduce_heads():
        def go():
            await_bytes(head_in.at[pl.ds(0, n - 1)], head_sems.at[1])
            head_sum[...] = jnp.sum(head_in[...], 0)
            head_all[me] = head_sum[...]
            spread(n, lambda peer: head_sum, head_all, head_sems.at[2], head_sems.at[3])

        when_reducer(go)

    def first_stage(k, _):
        other_line(k)
        send_y(k)
        return 0

    lax.fori_loop(1, L, first_stage, 0)

    def second_stage(k, _):
        for_sibling(k, 0)
        for_me(k, 0)
        return 0

    lax.fori_loop(0, L, second_stage, 0)

    def third_stage(k, _):
        t = target(k)
        up = goes_up(k)
        has_in = jnp.where(up, p.row > 0, p.row < L - 1)
        to = jnp.where(up, p.row + 1, p.row - 1)
        slot = jnp.where((t == to) & jnp.logical_not(up), L, t)
        for j, cut in enumerate(tiles):
            total = chip_sum(k, j)
            own[k, :, cut] = total

            @pl.when(has_in)
            def _():
                z_arrival(t, j).wait_recv()
                own[k, :, cut] += z_in[t, :, cut].astype(F32)

            z_out[k, :, cut] = own[k, :, cut].astype(BF16)
            z_copy(to, slot, k, j).start()

        @pl.when(k == 1)
        def _():
            reduce_heads()

        return 0

    lax.fori_loop(0, L - 1, third_stage, 0)
    for j, cut in enumerate(tiles):
        grad_ref[:, cut] = chip_sum(L - 1, j)

        @pl.when(p.row > 0)
        def _():
            z_arrival(p.row, j).wait_recv()
            grad_ref[:, cut] += z_in[p.row, :, cut].astype(F32)

        @pl.when(p.row < L - 1)
        def _():
            z_arrival(L, j).wait_recv()
            grad_ref[:, cut] += z_in[L, :, cut].astype(F32)

    if nb == n:
        await_bytes(head_all.at[pl.ds(0, nb - 1)], head_sems.at[3])
    else:
        @pl.when(is_reducer)
        def _():
            await_bytes(head_all.at[pl.ds(0, nb - 1)], head_sems.at[3])

        @pl.when(jnp.logical_not(is_reducer))
        def _():
            await_bytes(head_all.at[pl.ds(0, nb)], head_sems.at[3])

    for j in range(nb):
        headg_ref[:, j * LANES : (j + 1) * LANES] = head_all[j, 0 : nact + 1, :]
    stdg_ref[...] = head_all[0, nact + 1 : nact + 2, 0:nact]
    await_bytes(hid_ref.at[pl.ds(0, n - 1)], a2a_recv)
    stay.wait()
    await_bytes(send.at[pl.ds(0, n - 1)], a2a_send)
    await_bytes(held.at[pl.ds(0, last * shard), pl.ds(0, width - xw)], ring_send)
    await_bytes(held.at[pl.ds(0, last * shard), pl.ds(0, xw)], x_send)
    await_bytes(held.at[pl.ds(0, p.ring * shard)], sib_send)
    await_bytes(stats.at[pl.ds(0, n - 1)], stat_send)
    if nb == n:
        await_bytes(head_blk.at[pl.ds(0, nb - 1)], head_sems.at[0])
        await_bytes(head_in.at[pl.ds(0, n - 1)], head_sems.at[2])
    else:
        @pl.when(is_reducer)
        def _():
            await_bytes(head_blk.at[pl.ds(0, nb - 1)], head_sems.at[0])
            await_bytes(head_in.at[pl.ds(0, n - 1)], head_sems.at[2])

        @pl.when(jnp.logical_not(is_reducer))
        def _():
            await_bytes(head_blk.at[pl.ds(0, nb)], head_sems.at[0])

    await_bytes(sib_out, rs_sib_send)
    await_bytes(y_out, y_send)
    await_bytes(z_out.at[pl.ds(0, L - 1)], z_send)


def local(
    obs_feat, reward, value_old, done, minibatch_perm, old_mean, noise, gain_in, out_weight, head_weight, log_std
):
    rows, width = obs_feat.shape
    n = lax.axis_size("fsdp")
    steps = reward.shape[1]
    n_env = reward.shape[0]
    nact = log_std.shape[0]
    shard = out_weight.shape[0]
    block = max(shard, LANES)
    per = rows // n
    slot_rows = -(-per // 8) * 8
    L = n // 4
    ring = n // 2
    nb = min(n, width // LANES)
    vmem = pl.BlockSpec(memory_space=pltpu.VMEM)
    hbm = pl.BlockSpec(memory_space=pl.ANY)
    sem = pltpu.SemaphoreType.DMA
    V = pltpu.VMEM
    hid, grad, headg, stdg = pl.pallas_call(
        functools.partial(kernel, n, steps),
        name="step",
        out_shape=(
            V((n, slot_rows, width), BF16),
            V((shard, width), F32),
            V((nact + 1, width), F32),
            V((1, nact), F32),
        ),
        in_specs=[hbm, hbm] + [vmem] * 9,
        out_specs=(vmem, vmem, vmem, vmem),
        scratch_shapes=[
            V((rows, width), BF16),
            V((width, width), BF16),
            V((width // block, rows, block), BF16),
            V((rows, width), F32),
            V((rows, width), BF16),
            V((rows, width), BF16),
            V((n * slot_rows, rows), BF16),
            V((n, slot_rows, width), BF16),
            V((LANES, rows), F32),
            V((4, rows, LANES), F32),
            V((4, n_env, LANES), F32),
            V((LANES, width), F32),
            V((8, LANES), F32),
            V((n, 8, LANES), F32),
            V((8, LANES), F32),
            V((nb, 16, LANES), F32),
            V((n, 16, LANES), F32),
            V((16, LANES), F32),
            V((nb, 16, LANES), F32),
            V((2 * L, shard, width), BF16),
            V((2 * L, shard, width), BF16),
            V((L, shard, width), BF16),
            V((L, shard, width), BF16),
            V((L, shard, width), BF16),
            V((L + 1, shard, width), BF16),
            V((L, shard, width), F32),
            V((block, width // 4), F32),
            sem((3,)),
            sem(()),
            sem((ring, 4)),
            sem(()),
            sem((ring, 2)),
            sem((ring, 4)),
            sem((ring, 2)),
            sem(()),
            sem(()),
            sem(()),
            sem(()),
            sem(()),
            sem((4,)),
            sem(()),
            sem((2 * L, 4)),
            sem(()),
            sem((L, 4)),
            sem(()),
            sem((L + 1, 4)),
        ],
        compiler_params=pltpu.CompilerParams(
            collective_id=0, has_side_effects=True, vmem_limit_bytes=54 << 20
        ),
        cost_estimate=pl.CostEstimate(
            flops=4 * rows * width * width, bytes_accessed=16 * rows * width, transcendentals=0
        ),
    )(
        obs_feat, out_weight, gain_in[None, :], reward, value_old, done, minibatch_perm,
        old_mean.T, noise.T, head_weight.T, log_std[None, :],
    )
    hid = hid[:, :per].reshape(rows, width)
    return (hid, grad, headg.T, stdg[0])


def solution(mesh):
    both = P(("groups", "fsdp"), None)
    return jax.shard_map(
        local,
        mesh=mesh,
        in_specs=(
            both, both, both, both, P(("groups", "fsdp")), both, both, P(), P("fsdp", None), P(), P(),
        ),
        out_specs=(both, both, P("groups", None), P("groups")),
        check_vma=False,
    )
```

```python
import functools

import jax
import jax.numpy as jnp
from jax import lax
from jax.experimental import pallas as pl
from jax.experimental.pallas import tpu as pltpu
from jax.sharding import PartitionSpec as P

GAMMA = 0.99
LAMBDA_GAE = 0.95
CLIP_EPS = 0.2
NORM_EPS = 1e-05
MESH = pl.DeviceIdType.MESH
LANES = 128
F32 = jnp.float32
BF16 = jnp.bfloat16


def chip_at(pos, ring):
    half = ring // 2
    col = pos // half
    row = col * (ring - 1 - pos) + (1 - col) * pos
    return 2 * row + col


class Place:
    def __init__(self, n):
        self.n = n
        self.me = lax.axis_index("fsdp")
        self.group = lax.axis_index("groups")
        self.ring = n // 2
        self.rows = n // 4
        self.core = lax.rem(self.me, 2)
        chip = self.me // 2
        self.col = lax.rem(chip, 2)
        self.row = chip // 2
        self.pos = self.col * (self.ring - 1 - self.row) + (1 - self.col) * self.row
        self.step = 1 - 2 * self.core
        self.sibling = self.me + self.step

    def on_ring(self, ahead, core):
        pos = lax.rem(self.pos + ahead + self.ring, self.ring)
        return 2 * chip_at(pos, self.ring) + core

    def at(self, row, col, core):
        return (row * 2 + col) * 2 + core


def remote(src, dst, send, recv, device):
    return pltpu.make_async_remote_copy(
        src_ref=src, dst_ref=dst, send_sem=send, recv_sem=recv, device_id=device, device_id_type=MESH
    )


def await_bytes(part, sem):
    pltpu.make_async_copy(part, part, sem).wait()


def halves(start, size):
    first = (size // LANES + 1) // 2 * LANES
    return [(start, first), (start + first, size - first)]


def lanes(start, size):
    return pl.ds(pl.multiple_of(start, LANES), size)


def kernel(
    n, steps,
    x_hbm, w_hbm, gain_ref, reward_ref, value_ref, done_ref, perm_ref, mean_ref, noise_ref, head_ref, std_ref,
    hid_ref, grad_ref, headg_ref, stdg_ref,
    xv, held, normed, hidden, hnorm, ghid, place, send, rows_t, cols, envs, head, lstd,
    stats, stat_own, head_blk, head_in, head_sum, head_all,
    sib_out, sib_in, y_out, y_in, z_out, z_in, own, prod,
    load_sems, ring_send, ring_recv, x_send, x_recv, sibr_recv, sibx_recv, sib_send,
    stat_send, stat_recv, a2a_send, a2a_recv, head_sems,
    rs_sib_send, rs_sib_recv, y_send, y_recv, z_send, z_recv,
):
    p = Place(n)
    me, last, L = p.me, p.ring - 1, p.rows
    rows, width = xv.shape
    shard = w_hbm.shape[0]
    block = normed.shape[2]
    whole_blocks = shard == block
    nact = mean_ref.shape[0]
    n_env = reward_ref.shape[0]
    slot_rows = send.shape[1]
    per = rows // n
    tile = width // 4
    tiles = [pl.ds(j * tile, tile) for j in range(4)]
    total_rows = rows * n

    load_x = pltpu.make_async_copy(x_hbm, xv, load_sems.at[0])
    load_x.start()
    load_w = pltpu.make_async_copy(w_hbm, held.at[pl.ds(pl.multiple_of(me * shard, shard), shard)], load_sems.at[1])
    load_w.start()

    barrier = pltpu.get_barrier_semaphore()

    @pl.loop(1, n)
    def _(k):
        pl.semaphore_signal(barrier, inc=1, device_id={"fsdp": lax.rem(me + k, n)}, device_id_type=MESH)

    pl.semaphore_signal(barrier, inc=1, device_id={"groups": 1 - p.group}, device_id_type=MESH)
    pl.semaphore_wait(barrier, n)

    xw = width // LANES * 5 // 16 * LANES
    rest = width - 2 * xw
    ring_cuts = halves(p.group * (width - xw), xw) + halves(xw, rest)
    x_cuts = halves((1 - p.group) * (width - xw), xw)
    next_chip = {"fsdp": p.on_ring(p.step, p.core)}
    sibling = {"fsdp": p.sibling}
    partner = {"groups": 1 - p.group}

    def part(owner, cut):
        return held.at[pl.ds(pl.multiple_of(owner * shard, shard), shard), lanes(*cut)]

    def ring_copy(owner, s, i):
        ref = part(owner, ring_cuts[i])
        return remote(ref, ref, ring_send, ring_recv.at[s, i], next_chip)

    def x_copy(owner, s, i):
        ref = part(owner, ring_cuts[i])
        return remote(ref, ref, x_send, x_recv.at[s, i], partner)

    def x_arrival(owner, s, i):
        ref = part(owner, x_cuts[i])
        return remote(ref, ref, x_send, x_recv.at[s, i], partner)

    def sibr_copy(owner, s, i):
        ref = part(owner, ring_cuts[i])
        return remote(ref, ref, sib_send, sibr_recv.at[s, i], sibling)

    def sibx_copy(owner, s, i):
        ref = part(owner, x_cuts[i])
        return remote(ref, ref, sib_send, sibx_recv.at[s, i], sibling)

    def mine(s):
        return p.on_ring(-p.step * s, p.core)

    def theirs(s):
        return p.on_ring(p.step * s, 1 - p.core)

    load_w.wait()
    for i in range(4):
        ring_copy(me, 1, i).start()
    for i in range(4):
        sibr_copy(me, 0, i).start()
    for i in range(2):
        sibx_copy(me, 0, i).start()

    load_x.wait()
    square = jnp.zeros((rows, LANES), F32)
    for j in range(0, width, LANES):
        xf = xv[:, j : j + LANES].astype(F32)
        square = square + xf * xf
    scale_x = lax.rsqrt(jnp.sum(square, -1, keepdims=True) / width + NORM_EPS)
    for j in range(width // block):
        at = pl.ds(j * block, block)
        xf = xv[:, at].astype(F32)
        hidden[:, at] = xf
        normed[j] = (xf * scale_x * gain_ref[:, at]).astype(BF16)

    def add(index):
        for cut in tiles:
            hidden[:, cut] += jnp.dot(
                normed[index], held[pl.ds(pl.multiple_of(index * block, block), block), cut],
                preferred_element_type=F32,
            )

    def add_shard(owner):
        if whole_blocks:
            add(owner)

    def spread(count, source_of, dst, send_sem, recv_sem):
        @pl.loop(1, n)
        def _(k):
            peer = lax.rem(me + k, n)

            def go():
                remote(source_of(peer), dst.at[me], send_sem, recv_sem, {"fsdp": peer}).start()

            if count == n:
                go()
            else:
                pl.when(peer < count)(go)

    def advantages():
        lane = lax.broadcasted_iota(jnp.int32, (n_env, LANES), 1)
        envs[...] = jnp.zeros_like(envs)
        envs[0, :, 0:steps] = reward_ref[...]
        envs[1, :, 0 : steps + 1] = value_ref[...]
        envs[2, :, 0:steps] = 1.0 - done_ref[...].astype(F32)
        value, keep = envs[1], envs[2]
        ahead = pltpu.roll(value, LANES - 1, 1)
        gae = jnp.where(lane < steps, envs[0] + GAMMA * ahead * keep - value, 0.0)
        decay = GAMMA * LAMBDA_GAE * keep
        shift = 1
        while shift < steps:
            gae = gae + decay * pltpu.roll(gae, LANES - shift, 1)
            decay = decay * pltpu.roll(decay, LANES - shift, 1)
            shift *= 2
        envs[0] = gae
        envs[3] = gae + value
        spot = lax.broadcasted_iota(jnp.int32, (8, LANES), 1)
        stat_own[...] = jnp.where(spot == 0, jnp.sum(gae), jnp.where(spot == 1, jnp.sum(gae * gae), 0.0))
        stats[me] = stat_own[...]
        spread(n, lambda peer: stat_own, stats, stat_send, stat_recv)
        at_step = lax.broadcasted_iota(jnp.int32, (steps, LANES), 0) == lax.broadcasted_iota(
            jnp.int32, (steps, LANES), 1
        )
        for e in range(n_env):
            for c, k in ((0, 0), (1, 3)):
                line = jnp.broadcast_to(envs[k, e : e + 1, :], (steps, LANES))
                cols[c, e * steps : (e + 1) * steps, :] = jnp.broadcast_to(
                    jnp.sum(jnp.where(at_step, line, 0.0), -1, keepdims=True), (steps, LANES)
                )

    def placement():
        perm = perm_ref[...].reshape(1, rows)
        to = lax.div(perm, rows)
        slot = to * slot_rows + lax.rem(perm, per)
        place[...] = jnp.where(
            lax.broadcasted_iota(jnp.int32, place.shape, 0) == slot, 1.0, 0.0
        ).astype(BF16)

    def columns():
        for k, ref in ((0, mean_ref), (1, noise_ref)):
            rows_t[...] = jnp.zeros_like(rows_t)
            rows_t[0:nact] = ref[...].astype(F32)
            rows_t[16 : 16 + nact] = ref[...].astype(F32)
            cols[2 + k] = jnp.transpose(rows_t[...])
        head[...] = jnp.zeros_like(head)
        hf = head_ref[...].astype(F32)
        head[0 : nact + 1] = hf
        head[16 : 17 + nact] = hf
        lstd[...] = jnp.zeros_like(lstd)
        lstd[0:1, 0:nact] = std_ref[...]
        lstd[0:1, 16 : 16 + nact] = std_ref[...]

    def hop(s, _):
        owner = mine(s)
        for i in range(4):
            ring_copy(owner, s, i).wait_recv()

            @pl.when(s < last)
            def _():
                ring_copy(owner, s + 1, i).start()

            if i < 2:
                x_copy(owner, s, i).start()
            sibr_copy(owner, s, i).start()
        before = mine(s - 1)

        @pl.when(s > 1)
        def _():
            for i in range(2):
                x_arrival(before, s - 1, i).wait_recv()
                sibx_copy(before, s - 1, i).start()

        add_shard(before)

        @pl.when(s == 1)
        def _():
            advantages()

        @pl.when(s == 2)
        def _():
            placement()

        @pl.when(s == 3)
        def _():
            columns()

        @pl.when(s > 1)
        def _():
            other = theirs(s - 2)
            for i in range(4):
                sibr_copy(other, s - 2, i).wait_recv()
            for i in range(2):
                sibx_copy(other, s - 2, i).wait_recv()
            add_shard(other)

        return 0

    lax.fori_loop(1, p.ring, hop, 0)
    def term(index, cut):
        rows_at = pl.ds(pl.multiple_of(index * block, block), block)
        return jnp.dot(normed[index], held[rows_at, lanes(*cut)], preferred_element_type=F32)

    def last_x():
        for i in range(2):
            x_arrival(mine(last), last, i).wait_recv()
            sibx_copy(mine(last), last, i).start()

    def await_sibling(s, ring_part, x_part):
        if ring_part:
            for i in range(4):
                sibr_copy(theirs(s), s, i).wait_recv()
        if x_part:
            for i in range(2):
                sibx_copy(theirs(s), s, i).wait_recv()

    await_sibling(last - 1, True, True)
    if whole_blocks:
        pair = (mine(last), theirs(last))
        add(theirs(last - 1))
    else:
        last_x()
        await_sibling(last, True, True)
        lax.fori_loop(0, width // block - 2, lambda b, _: (add(b), 0)[1], 0)
        pair = (width // block - 2, width // block - 1)

    def finish(cut, square):
        h = hidden[:, lanes(*cut)] + term(pair[0], cut) + term(pair[1], cut)
        hidden[:, lanes(*cut)] = h
        for j in range(0, cut[1], LANES):
            piece = h[:, j : j + LANES]
            square = square + piece * piece
        moved = jnp.dot(place[...], h.astype(BF16), preferred_element_type=F32).astype(BF16)
        send[:, :, lanes(*cut)] = moved.reshape(n, slot_rows, cut[1])
        return square

    ring_part = (p.group * xw, width - xw)
    x_part = ((1 - p.group) * (width - xw), xw)

    def row_copy(peer, cut):
        return remote(
            send.at[peer, :, lanes(*cut)], hid_ref.at[me, :, lanes(*cut)], a2a_send, a2a_recv, {"fsdp": peer}
        )

    def same_line(cut):
        row_copy(p.sibling, cut).start()

        @pl.loop(1, L)
        def _(k):
            to = lax.rem(p.row + k, L)
            row_copy(p.at(to, p.col, 0), cut).start()
            row_copy(p.at(to, p.col, 1), cut).start()

    def other_line(m, cut):
        to = lax.rem(p.row + L // 2 + m, L)
        row_copy(p.at(to, 1 - p.col, 0), cut).start()
        row_copy(p.at(to, 1 - p.col, 1), cut).start()

    square = jnp.zeros((rows, LANES), F32)
    for i, cut in enumerate(ring_cuts):
        if whole_blocks:
            sibr_copy(theirs(last), last, i).wait_recv()
        square = finish(cut, square)

    @pl.loop(0, L - 1)
    def _(m):
        other_line(m, ring_part)

    same_line(ring_part)
    if whole_blocks:
        last_x()
    for i, cut in enumerate(x_cuts):
        if whole_blocks:
            sibx_copy(theirs(last), last, i).wait_recv()
        square = finish(cut, square)
    same_line(x_part)
    stay = pltpu.make_async_copy(send.at[me], hid_ref.at[me], load_sems.at[2])
    stay.start()

    rinv = lax.rsqrt(jnp.sum(square, -1, keepdims=True) / width + NORM_EPS)
    headb = head[...].astype(BF16)
    heads = jnp.zeros((rows, LANES), F32)
    for j, cut in enumerate(tiles):
        hb = (hidden[:, cut] * rinv).astype(BF16)
        hnorm[:, cut] = hb
        heads = heads + lax.dot_general(
            hb, headb[:, j * tile : (j + 1) * tile], (((1,), (1,)), ((), ())), preferred_element_type=F32
        )
    await_bytes(stats.at[pl.ds(0, n - 1)], stat_recv)
    sums = jnp.sum(stats[...], 0)
    mean_adv = sums[0:1, 0:1] / total_rows
    var_adv = sums[0:1, 1:2] / total_rows - mean_adv * mean_adv
    advant = ((cols[0, :, 0:1] - mean_adv) * lax.rsqrt(var_adv + NORM_EPS)).astype(BF16).astype(F32)
    ret = cols[1, :, 0:1].astype(BF16).astype(F32)
    lane = lax.broadcasted_iota(jnp.int32, (1, LANES), 1)
    one = lax.rem(lane, 16)
    first = lane < 16
    is_act = (one < nact) & (lane < 32)
    is_value = (one == nact) & (lane < 32)
    inv = jnp.where(is_act, jnp.exp(-lstd[0:1, :]), 0.0)
    noise = cols[3]
    u = (cols[2] - heads) * inv
    logr = jnp.sum(jnp.where(first, -noise * u - 0.5 * u * u, 0.0), -1, keepdims=True)
    ratio = jnp.exp(logr)
    scale = 1.0 / jnp.sqrt(jnp.full((1, 1), total_rows, F32))
    clipped = jnp.clip(ratio, 1.0 - CLIP_EPS, 1.0 + CLIP_EPS)
    active = ratio * advant <= clipped * advant
    glogr = jnp.where(active, -scale * advant, 0.0) * ratio
    ghead = jnp.where(is_value, scale * (heads - ret), glogr * (inv * (noise + u)))
    std_part = jnp.sum(glogr * (noise * u + u * u), 0, keepdims=True)
    along = jnp.sum(jnp.where(first, ghead * heads, 0.0), -1, keepdims=True) / width
    pull = rinv * rinv * along

    def two_parts(value):
        high = value.astype(BF16)
        return jnp.where(first, high.astype(F32), value - high.astype(F32)).astype(BF16)

    gscaled = two_parts(ghead * rinv)
    for j, cut in enumerate(tiles):
        g = jnp.dot(gscaled, headb[:, j * tile : (j + 1) * tile], preferred_element_type=F32)
        ghid[:, cut] = (g - hidden[:, cut] * pull).astype(BF16)

    def product(owner, cut):
        index = owner if whole_blocks else owner * shard // block
        value = lax.dot_general(
            normed[index], ghid[:, cut], (((0,), (0,)), ((), ())), preferred_element_type=F32
        )
        if whole_blocks:
            return value
        prod[...] = value
        return prod[pl.ds(pl.multiple_of(lax.rem(owner * shard, block), shard), shard)]

    def goes_up(k):
        up_first = 2 * p.row < L
        return jnp.where(up_first, k < L - 1 - p.row, (k >= p.row) & (k < L - 1))

    def target(k):
        ups, downs = L - 1 - p.row, p.row
        up_first = 2 * p.row < L
        up_at = jnp.where(up_first, k, k - downs)
        down_at = jnp.where(up_first, k - ups, k)
        up = goes_up(k)
        return jnp.where(up, L - 1 - up_at, jnp.where(k < L - 1, down_at, p.row))

    def sib_copy(slot, j):
        return remote(
            sib_out.at[slot, :, tiles[j]], sib_in.at[slot, :, tiles[j]], rs_sib_send, rs_sib_recv.at[slot, j], sibling
        )

    def y_copy(k, j):
        return remote(
            y_out.at[k, :, tiles[j]], y_in.at[k, :, tiles[j]], y_send, y_recv.at[k, j],
            {"fsdp": p.at(p.row, 1 - p.col, p.core)},
        )

    def for_sibling(k, cross):
        slot = 2 * k + cross
        owner = p.at(target(k), (1 - p.col) if cross else p.col, 1 - p.core)
        for j, cut in enumerate(tiles):
            sib_out[slot, :, cut] = product(owner, cut).astype(BF16)
            sib_copy(slot, j).start()

    def for_me(k, cross):
        owner = p.at(target(k), (1 - p.col) if cross else p.col, p.core)
        for cut in tiles:
            own[k, :, cut] = product(owner, cut)

    def send_y(k):
        for_sibling(k, 1)
        for_me(k, 1)
        for j, cut in enumerate(tiles):
            sib_copy(2 * k + 1, j).wait_recv()
            y_out[k, :, cut] = (own[k, :, cut] + sib_in[2 * k + 1, :, cut].astype(F32)).astype(BF16)
            y_copy(k, j).start()

    def chip_sum(k, j):
        cut = tiles[j]
        sib_copy(2 * k, j).wait_recv()
        y_copy(k, j).wait_recv()
        return own[k, :, cut] + sib_in[2 * k, :, cut].astype(F32) + y_in[k, :, cut].astype(F32)

    def z_copy(to, slot, k, j):
        return remote(
            z_out.at[k, :, tiles[j]], z_in.at[slot, :, tiles[j]], z_send, z_recv.at[slot, j],
            {"fsdp": p.at(to, p.col, p.core)},
        )

    def z_arrival(slot, j):
        return remote(
            z_out.at[0, :, tiles[j]], z_in.at[slot, :, tiles[j]], z_send, z_recv.at[slot, j],
            {"fsdp": p.sibling},
        )

    send_y(0)
    other_line(0, x_part)

    gparts = two_parts(ghead)
    row = lax.broadcasted_iota(jnp.int32, (16, LANES), 0)
    for j, cut in enumerate(tiles):
        part_sum = lax.dot_general(gparts, hnorm[:, cut], (((0,), (0,)), ((), ())), preferred_element_type=F32)
        both = part_sum[0:16] + part_sum[16:32]
        for i in range(tile // LANES):
            head_blk[j * (tile // LANES) + i] = jnp.where(
                row == nact + 1, std_part, both[:, i * LANES : (i + 1) * LANES]
            )
    nb = head_all.shape[0]
    is_reducer = me < nb

    def when_reducer(go):
        if nb == n:
            go()
        else:
            pl.when(is_reducer)(go)

    def keep_block():
        head_in[me] = head_blk[me]

    when_reducer(keep_block)
    spread(nb, lambda peer: head_blk.at[peer], head_in, head_sems.at[0], head_sems.at[1])

    def reduce_heads():
        def go():
            await_bytes(head_in.at[pl.ds(0, n - 1)], head_sems.at[1])
            head_sum[...] = jnp.sum(head_in[...], 0)
            head_all[me] = head_sum[...]
            spread(n, lambda peer: head_sum, head_all, head_sems.at[2], head_sems.at[3])

        when_reducer(go)

    def first_stage(k, _):
        @pl.when(k == 1)
        def _():
            other_line(L - 1, ring_part)

        other_line(k, x_part)
        send_y(k)
        return 0

    lax.fori_loop(1, L, first_stage, 0)

    def second_stage(k, _):
        for_sibling(k, 0)
        for_me(k, 0)
        return 0

    lax.fori_loop(0, L, second_stage, 0)

    def third_stage(k, _):
        t = target(k)
        up = goes_up(k)
        has_in = jnp.where(up, p.row > 0, p.row < L - 1)
        to = jnp.where(up, p.row + 1, p.row - 1)
        slot = jnp.where((t == to) & jnp.logical_not(up), L, t)
        for j, cut in enumerate(tiles):
            total = chip_sum(k, j)
            own[k, :, cut] = total

            @pl.when(has_in)
            def _():
                z_arrival(t, j).wait_recv()
                own[k, :, cut] += z_in[t, :, cut].astype(F32)

            z_out[k, :, cut] = own[k, :, cut].astype(BF16)
            z_copy(to, slot, k, j).start()

        @pl.when(k == 1)
        def _():
            reduce_heads()

        return 0

    lax.fori_loop(0, L - 1, third_stage, 0)
    for j, cut in enumerate(tiles):
        grad_ref[:, cut] = chip_sum(L - 1, j)

        @pl.when(p.row > 0)
        def _():
            z_arrival(p.row, j).wait_recv()
            grad_ref[:, cut] += z_in[p.row, :, cut].astype(F32)

        @pl.when(p.row < L - 1)
        def _():
            z_arrival(L, j).wait_recv()
            grad_ref[:, cut] += z_in[L, :, cut].astype(F32)

    if nb == n:
        await_bytes(head_all.at[pl.ds(0, nb - 1)], head_sems.at[3])
    else:
        @pl.when(is_reducer)
        def _():
            await_bytes(head_all.at[pl.ds(0, nb - 1)], head_sems.at[3])

        @pl.when(jnp.logical_not(is_reducer))
        def _():
            await_bytes(head_all.at[pl.ds(0, nb)], head_sems.at[3])

    for j in range(nb):
        headg_ref[:, j * LANES : (j + 1) * LANES] = head_all[j, 0 : nact + 1, :]
    stdg_ref[...] = head_all[0, nact + 1 : nact + 2, 0:nact]
    await_bytes(hid_ref.at[pl.ds(0, n - 1)], a2a_recv)
    stay.wait()
    await_bytes(send.at[pl.ds(0, n - 1)], a2a_send)
    await_bytes(held.at[pl.ds(0, last * shard), pl.ds(0, width - xw)], ring_send)
    await_bytes(held.at[pl.ds(0, last * shard), pl.ds(0, xw)], x_send)
    await_bytes(held.at[pl.ds(0, p.ring * shard)], sib_send)
    await_bytes(stats.at[pl.ds(0, n - 1)], stat_send)
    if nb == n:
        await_bytes(head_blk.at[pl.ds(0, nb - 1)], head_sems.at[0])
        await_bytes(head_in.at[pl.ds(0, n - 1)], head_sems.at[2])
    else:
        @pl.when(is_reducer)
        def _():
            await_bytes(head_blk.at[pl.ds(0, nb - 1)], head_sems.at[0])
            await_bytes(head_in.at[pl.ds(0, n - 1)], head_sems.at[2])

        @pl.when(jnp.logical_not(is_reducer))
        def _():
            await_bytes(head_blk.at[pl.ds(0, nb)], head_sems.at[0])

    await_bytes(sib_out, rs_sib_send)
    await_bytes(y_out, y_send)
    await_bytes(z_out.at[pl.ds(0, L - 1)], z_send)


def store_kernel(a, b, c, d, a_out, b_out, c_out, d_out, sems):
    copies = [
        pltpu.make_async_copy(src, dst, sems.at[i])
        for i, (src, dst) in enumerate(((a, a_out), (b, b_out), (c, c_out), (d, d_out)))
    ]
    for copy in copies:
        copy.start()
    for copy in copies:
        copy.wait()


def local(
    obs_feat, reward, value_old, done, minibatch_perm, old_mean, noise, gain_in, out_weight, head_weight, log_std
):
    rows, width = obs_feat.shape
    n = lax.axis_size("fsdp")
    steps = reward.shape[1]
    n_env = reward.shape[0]
    nact = log_std.shape[0]
    shard = out_weight.shape[0]
    block = max(shard, LANES)
    per = rows // n
    slot_rows = -(-per // 8) * 8
    L = n // 4
    ring = n // 2
    nb = min(n, width // LANES)
    vmem = pl.BlockSpec(memory_space=pltpu.VMEM)
    hbm = pl.BlockSpec(memory_space=pl.ANY)
    sem = pltpu.SemaphoreType.DMA
    V = pltpu.VMEM
    hid, grad, headg, stdg = pl.pallas_call(
        functools.partial(kernel, n, steps),
        name="step",
        out_shape=(
            V((n, slot_rows, width), BF16),
            V((shard, width), F32),
            V((nact + 1, width), F32),
            V((1, nact), F32),
        ),
        in_specs=[hbm, hbm] + [vmem] * 9,
        out_specs=(vmem, vmem, vmem, vmem),
        scratch_shapes=[
            V((rows, width), BF16),
            V((width, width), BF16),
            V((width // block, rows, block), BF16),
            V((rows, width), F32),
            V((rows, width), BF16),
            V((rows, width), BF16),
            V((n * slot_rows, rows), BF16),
            V((n, slot_rows, width), BF16),
            V((LANES, rows), F32),
            V((4, rows, LANES), F32),
            V((4, n_env, LANES), F32),
            V((LANES, width), F32),
            V((8, LANES), F32),
            V((n, 8, LANES), F32),
            V((8, LANES), F32),
            V((nb, 16, LANES), F32),
            V((n, 16, LANES), F32),
            V((16, LANES), F32),
            V((nb, 16, LANES), F32),
            V((2 * L, shard, width), BF16),
            V((2 * L, shard, width), BF16),
            V((L, shard, width), BF16),
            V((L, shard, width), BF16),
            V((L, shard, width), BF16),
            V((L + 1, shard, width), BF16),
            V((L, shard, width), F32),
            V((block, width // 4), F32),
            sem((3,)),
            sem(()),
            sem((ring, 4)),
            sem(()),
            sem((ring, 2)),
            sem((ring, 4)),
            sem((ring, 2)),
            sem(()),
            sem(()),
            sem(()),
            sem(()),
            sem(()),
            sem((4,)),
            sem(()),
            sem((2 * L, 4)),
            sem(()),
            sem((L, 4)),
            sem(()),
            sem((L + 1, 4)),
        ],
        compiler_params=pltpu.CompilerParams(
            collective_id=0, has_side_effects=True, vmem_limit_bytes=54 << 20
        ),
        cost_estimate=pl.CostEstimate(
            flops=4 * rows * width * width, bytes_accessed=16 * rows * width, transcendentals=0
        ),
    )(
        obs_feat, out_weight, gain_in[None, :], reward, value_old, done, minibatch_perm,
        old_mean.T, noise.T, head_weight.T, log_std[None, :],
    )
    results = (hid, grad, headg, stdg)
    hid, grad, headg, stdg = pl.pallas_call(
        store_kernel,
        name="store",
        out_shape=tuple(jax.ShapeDtypeStruct(r.shape, r.dtype) for r in results),
        in_specs=[hbm] * 4,
        out_specs=(hbm,) * 4,
        scratch_shapes=[sem((4,))],
        compiler_params=pltpu.CompilerParams(vmem_limit_bytes=1 << 20),
    )(*results)
    hid = hid[:, :per].reshape(rows, width)
    return (hid, grad, headg.T, stdg[0])


def solution(mesh):
    both = P(("groups", "fsdp"), None)
    return jax.shard_map(
        local,
        mesh=mesh,
        in_specs=(
            both, both, both, both, P(("groups", "fsdp")), both, both, P(), P("fsdp", None), P(), P(),
        ),
        out_specs=(both, both, P("groups", None), P("groups")),
        check_vma=False,
    )
```

```python
import functools

import jax
import jax.numpy as jnp
from jax import lax
from jax.experimental import pallas as pl
from jax.experimental.pallas import tpu as pltpu
from jax.sharding import PartitionSpec as P

GAMMA = 0.99
LAMBDA_GAE = 0.95
CLIP_EPS = 0.2
NORM_EPS = 1e-05
MESH = pl.DeviceIdType.MESH
LANES = 128
F32 = jnp.float32
BF16 = jnp.bfloat16


class Place:
    def __init__(self, n):
        self.me = lax.axis_index("fsdp")
        self.group = lax.axis_index("groups")
        self.rows = n // 4
        self.core = lax.rem(self.me, 2)
        chip = self.me // 2
        self.col = lax.rem(chip, 2)
        self.row = chip // 2
        self.sibling = self.me + 1 - 2 * self.core
        self.across = self.at(self.row, 1 - self.col, self.core)
        self.at_end = (self.row == 0) | (self.row == self.rows - 1)

    def at(self, row, col, core):
        return (row * 2 + col) * 2 + core

    def nth_row(self, q):
        below, above = self.row, self.rows - 1 - self.row
        near = jnp.minimum(below, above)
        toward = jnp.where(below < above, 1, -1)
        inner = self.row + toward * jnp.where(lax.rem(q, 2) == 1, -((q + 1) // 2), q // 2)
        outer = self.row + toward * (q - near)
        return jnp.where(q <= 2 * near, inner, outer)


def remote(src, dst, send, recv, device):
    return pltpu.make_async_remote_copy(
        src_ref=src, dst_ref=dst, send_sem=send, recv_sem=recv, device_id=device, device_id_type=MESH
    )


def await_bytes(part, sem):
    pltpu.make_async_copy(part, part, sem).wait()


def cuts_of(start, size, count):
    blocks, cuts = size // LANES, []
    for i in range(count):
        take = -(-blocks // (count - i))
        cuts.append((start, take * LANES))
        start, blocks = start + take * LANES, blocks - take
    return cuts


def lanes(start, size):
    return pl.ds(pl.multiple_of(start, LANES), size)


def kernel(
    n, steps,
    x_hbm, w_hbm, gain_ref, reward_ref, value_ref, done_ref, perm_ref, mean_ref, noise_ref, head_ref, std_ref,
    hid_ref, grad_ref, headg_ref, stdg_ref,
    xv, held, normed, hidden, hnorm, ghid, place, send, rows_t, cols, envs, head, lstd,
    stats, stat_own, head_blk, head_in, head_sum, head_all,
    sib_out, sib_in, y_out, y_in, z_out, z_in, zq_out, zq_in, yq_out, yq_in, own, ownz, normed_t, layer,
    obs_send, ext_in, ext_out, normed_e,
    load_sems, z_ag_send, z_ag_recv, y_ag_send, y_ag_recv, x_send, x_recv, sibr_recv, sibx_recv, sib_send,
    ext_send, ext_recv, fwd_send,
    stat_send, stat_recv, a2a_send, a2a_recv, head_sems,
    rs_sib_send, rs_sib_recv, y_send, y_recv, z_send, z_recv, zq_send, zq_recv, yq_send, yq_recv,
):
    p = Place(n)
    me, L = p.me, p.rows
    rows, width = xv.shape
    shard = w_hbm.shape[0]
    block = normed.shape[2]
    whole_blocks = shard == block
    nact = mean_ref.shape[0]
    n_env = reward_ref.shape[0]
    slot_rows = send.shape[1]
    per = rows // n
    tile = width // 4
    tiles = [pl.ds(j * tile, tile) for j in range(4)]
    total_rows = rows * n

    load_x = pltpu.make_async_copy(x_hbm, xv, load_sems.at[0])
    load_x.start()
    load_w = pltpu.make_async_copy(w_hbm, held.at[pl.ds(pl.multiple_of(me * shard, shard), shard)], load_sems.at[1])
    load_w.start()

    ext_in[...] = jnp.zeros_like(ext_in)
    barrier = pltpu.get_barrier_semaphore()

    @pl.loop(1, n)
    def _(k):
        pl.semaphore_signal(barrier, inc=1, device_id={"fsdp": lax.rem(me + k, n)}, device_id_type=MESH)

    pl.semaphore_signal(barrier, inc=1, device_id={"groups": 1 - p.group}, device_id_type=MESH)

    perm = perm_ref[...].reshape(1, rows)
    slot_of = lax.div(perm, rows) * slot_rows + lax.rem(perm, per)
    place[...] = jnp.where(lax.broadcasted_iota(jnp.int32, place.shape, 0) == slot_of, 1.0, 0.0).astype(BF16)
    load_x.wait()

    @pl.when(p.at_end)
    def _():
        for cut in tiles:
            moved = jnp.dot(place[...], xv[:, cut], preferred_element_type=F32).astype(BF16)
            obs_send[:, :, cut] = moved.reshape(n, slot_rows, tile)

    pl.semaphore_wait(barrier, n)

    xw = width // LANES * 5 // 16 * LANES
    rest = width - 2 * xw
    ring_cuts = cuts_of(p.group * (width - xw), xw, 2) + cuts_of(xw, rest, 2)
    x_cuts = cuts_of((1 - p.group) * (width - xw), xw, 2)
    sibling = {"fsdp": p.sibling}
    partner = {"groups": 1 - p.group}
    across = {"fsdp": p.across}

    def owner(row, line, core):
        return p.at(row, p.col if line == 0 else 1 - p.col, core)

    def part(device, cut):
        return held.at[pl.ds(pl.multiple_of(device * shard, shard), shard), lanes(*cut)]

    def z_ag(o, i, to):
        ref = part(owner(o, 0, p.core), ring_cuts[i])
        return remote(ref, ref, z_ag_send, z_ag_recv.at[o, i], {"fsdp": p.at(to, p.col, p.core)})

    def y_ag(o, line, i):
        ref = part(owner(o, line, p.core), ring_cuts[i])
        return remote(ref, ref, y_ag_send, y_ag_recv.at[o, i], across)

    def x_ag(o, line, i, cuts):
        ref = part(owner(o, line, p.core), cuts[i])
        return remote(ref, ref, x_send, x_recv.at[2 * o + line, i], partner)

    def sibr(o, line, i, core):
        ref = part(owner(o, line, core), ring_cuts[i])
        return remote(ref, ref, sib_send, sibr_recv.at[2 * o + line, i], sibling)

    def sibx(o, line, i, core):
        ref = part(owner(o, line, core), x_cuts[i])
        return remote(ref, ref, sib_send, sibx_recv.at[2 * o + line, i], sibling)

    def ext_copies(to):
        for core in range(2):
            for kind in range(2):
                block_of = p.at(to, p.col if kind == 0 else 1 - p.col, core)
                slot = (jnp.where(p.row > 0, 2, 0) + p.core) * 2 + kind
                remote(
                    obs_send.at[block_of], ext_in.at[slot], ext_send, ext_recv,
                    {"fsdp": p.at(to, p.col, core)},
                ).start()

    load_w.wait()
    for i in range(4):
        @pl.when(p.row > 0)
        def _():
            z_ag(p.row, i, p.row - 1).start()

        @pl.when(p.row < L - 1)
        def _():
            z_ag(p.row, i, p.row + 1).start()

        y_ag(p.row, 0, i).start()
    for i in range(4):
        sibr(p.row, 0, i, p.core).start()
    for i in range(2):
        sibx(p.row, 0, i, p.core).start()

    @pl.when(p.at_end)
    def _():
        ext_copies(jnp.where(p.row > 0, p.row - 1, p.row + 1))

    square = jnp.zeros((rows, LANES), F32)
    for j in range(0, width, LANES):
        xf = xv[:, j : j + LANES].astype(F32)
        square = square + xf * xf
    scale_x = lax.rsqrt(jnp.sum(square, -1, keepdims=True) / width + NORM_EPS)
    for j in range(width // block):
        at = pl.ds(j * block, block)
        xf = xv[:, at].astype(F32)
        hidden[:, at] = xf
        normed[j] = (xf * scale_x * gain_ref[:, at]).astype(BF16)

    def add(index):
        for cut in tiles:
            hidden[:, cut] += jnp.dot(
                normed[index], held[pl.ds(pl.multiple_of(index * block, block), block), cut],
                preferred_element_type=F32,
            )

    def add_shard(device):
        if whole_blocks:
            add(device)

    def spread(count, source_of, dst, send_sem, recv_sem):
        @pl.loop(1, n)
        def _(k):
            peer = lax.rem(me + k, n)

            def go():
                remote(source_of(peer), dst.at[me], send_sem, recv_sem, {"fsdp": peer}).start()

            if count == n:
                go()
            else:
                pl.when(peer < count)(go)

    def advantages():
        lane = lax.broadcasted_iota(jnp.int32, (n_env, LANES), 1)
        envs[...] = jnp.zeros_like(envs)
        envs[0, :, 0:steps] = reward_ref[...]
        envs[1, :, 0 : steps + 1] = value_ref[...]
        envs[2, :, 0:steps] = 1.0 - done_ref[...].astype(F32)
        value, keep = envs[1], envs[2]
        ahead = pltpu.roll(value, LANES - 1, 1)
        gae = jnp.where(lane < steps, envs[0] + GAMMA * ahead * keep - value, 0.0)
        decay = GAMMA * LAMBDA_GAE * keep
        shift = 1
        while shift < steps:
            gae = gae + decay * pltpu.roll(gae, LANES - shift, 1)
            decay = decay * pltpu.roll(decay, LANES - shift, 1)
            shift *= 2
        envs[0] = gae
        envs[3] = gae + value
        spot = lax.broadcasted_iota(jnp.int32, (8, LANES), 1)
        stat_own[...] = jnp.where(spot == 0, jnp.sum(gae), jnp.where(spot == 1, jnp.sum(gae * gae), 0.0))
        stats[me] = stat_own[...]
        spread(n, lambda peer: stat_own, stats, stat_send, stat_recv)
        at_step = lax.broadcasted_iota(jnp.int32, (steps, LANES), 0) == lax.broadcasted_iota(
            jnp.int32, (steps, LANES), 1
        )
        for e in range(n_env):
            for c, k in ((0, 0), (1, 3)):
                line = jnp.broadcast_to(envs[k, e : e + 1, :], (steps, LANES))
                cols[c, e * steps : (e + 1) * steps, :] = jnp.broadcast_to(
                    jnp.sum(jnp.where(at_step, line, 0.0), -1, keepdims=True), (steps, LANES)
                )

    def columns():
        for k, ref in ((0, mean_ref), (1, noise_ref)):
            rows_t[...] = jnp.zeros_like(rows_t)
            rows_t[0:nact] = ref[...].astype(F32)
            rows_t[16 : 16 + nact] = ref[...].astype(F32)
            cols[2 + k] = jnp.transpose(rows_t[...])
        for j in range(width // block):
            normed_t[j * block : (j + 1) * block] = jnp.transpose(normed[j].astype(F32)).astype(BF16)
        head[...] = jnp.zeros_like(head)
        hf = head_ref[...].astype(F32)
        head[0 : nact + 1] = hf
        head[16 : 17 + nact] = hf
        lstd[...] = jnp.zeros_like(lstd)
        lstd[0:1, 0:nact] = std_ref[...]
        lstd[0:1, 16 : 16 + nact] = std_ref[...]

    def z_arrives(o):
        to = jnp.where(o < p.row, p.row + 1, p.row - 1)
        for i in range(4):
            z_ag(o, i, p.row).wait_recv()

            @pl.when((to >= 0) & (to < L))
            def _():
                z_ag(o, i, to).start()

            y_ag(o, 0, i).start()
            if i < 2:
                x_ag(o, 0, i, ring_cuts).start()
            sibr(o, 0, i, p.core).start()

    def y_arrives(o, pieces):
        for i in pieces:
            y_ag(o, 1, i).wait_recv()
            if i < 2:
                x_ag(o, 1, i, ring_cuts).start()
            sibr(o, 1, i, p.core).start()

    def x_arrives(o, line):
        for i in range(2):
            x_ag(o, line, i, x_cuts).wait_recv()
            sibx(o, line, i, p.core).start()

    def sib_arrives(o, line):
        for i in range(4):
            sibr(o, line, i, 1 - p.core).wait_recv()
        for i in range(2):
            sibx(o, line, i, 1 - p.core).wait_recv()

    def hop(q, _):
        z_arrives(p.nth_row(q))
        y_arrives(p.nth_row(q - 1), range(4))
        before = p.nth_row(q - 1)

        @pl.when(q > 1)
        def _():
            x_arrives(before, 0)

        add_shard(owner(before, 0, p.core))

        @pl.when(q == 1)
        def _():
            advantages()

        @pl.when((q == 2) & p.at_end)
        def _():
            @pl.loop(2, L)
            def _(k):
                ext_copies(jnp.where(p.row > 0, p.row - k, p.row + k))

        @pl.when(q == 2)
        def _():
            columns()

        @pl.when(q > 1)
        def _():
            o = p.nth_row(q - 2)
            x_arrives(o, 1)
            add_shard(owner(o, 1, p.core))
            sib_arrives(o, 0)
            add_shard(owner(o, 0, 1 - p.core))

        @pl.when(q > 2)
        def _():
            o = p.nth_row(q - 3)
            sib_arrives(o, 1)
            add_shard(owner(o, 1, 1 - p.core))

        return 0

    lax.fori_loop(1, L, hop, 0)

    def term(index, cut):
        rows_at = pl.ds(pl.multiple_of(index * block, block), block)
        return jnp.dot(normed[index], held[rows_at, lanes(*cut)], preferred_element_type=F32)

    far, farther, farthest = p.nth_row(L - 3), p.nth_row(L - 2), p.nth_row(L - 1)
    sib_arrives(farther, 0)
    add_shard(owner(farther, 0, 1 - p.core))
    sib_arrives(far, 1)
    add_shard(owner(far, 1, 1 - p.core))
    y_arrives(farthest, (0, 1))
    x_arrives(farthest, 0)
    add_shard(owner(farthest, 0, p.core))
    x_arrives(farther, 1)
    add_shard(owner(farther, 1, p.core))
    sib_arrives(farthest, 0)
    add_shard(owner(farthest, 0, 1 - p.core))
    sib_arrives(farther, 1)
    add_shard(owner(farther, 1, 1 - p.core))
    y_arrives(farthest, (2, 3))
    if whole_blocks:
        pair = (owner(farthest, 1, p.core), owner(farthest, 1, 1 - p.core))
    else:
        x_arrives(farthest, 1)
        sib_arrives(farthest, 1)
        lax.fori_loop(0, width // block - 2, lambda b, _: (add(b), 0)[1], 0)
        pair = (width // block - 2, width // block - 1)

    def finish(cut, square):
        h = hidden[:, lanes(*cut)] + term(pair[0], cut) + term(pair[1], cut)
        hidden[:, lanes(*cut)] = h
        for j in range(0, cut[1], LANES):
            piece = h[:, j : j + LANES]
            square = square + piece * piece
        moved = jnp.dot(place[...], h.astype(BF16), preferred_element_type=F32).astype(BF16)
        send[:, :, lanes(*cut)] = moved.reshape(n, slot_rows, cut[1])
        return square

    ring_part = (p.group * xw, width - xw)
    x_part = ((1 - p.group) * (width - xw), xw)

    def row_copy(peer, cut):
        return remote(
            send.at[peer, :, lanes(*cut)], hid_ref.at[me, :, lanes(*cut)], a2a_send, a2a_recv, {"fsdp": peer}
        )

    def same_line(cut):
        row_copy(p.sibling, cut).start()

        @pl.when(jnp.logical_not(p.at_end))
        def _():
            @pl.loop(1, L)
            def _(k):
                to = lax.rem(p.row + k, L)
                row_copy(p.at(to, p.col, 0), cut).start()
                row_copy(p.at(to, p.col, 1), cut).start()

    def other_line(m, cut):
        to = lax.rem(p.row + L // 2 + m, L)

        @pl.when(jnp.logical_not(p.at_end) | (to == p.row))
        def _():
            row_copy(p.at(to, 1 - p.col, 0), cut).start()
            row_copy(p.at(to, 1 - p.col, 1), cut).start()

    square = jnp.zeros((rows, LANES), F32)
    for i, cut in enumerate(ring_cuts):
        if whole_blocks:
            sibr(farthest, 1, i, 1 - p.core).wait_recv()
        square = finish(cut, square)

    @pl.loop(0, L - 1)
    def _(m):
        other_line(m, ring_part)

    same_line(ring_part)
    if whole_blocks:
        x_arrives(farthest, 1)
    for i, cut in enumerate(x_cuts):
        if whole_blocks:
            sibx(farthest, 1, i, 1 - p.core).wait_recv()
        square = finish(cut, square)
    same_line(x_part)
    stay = pltpu.make_async_copy(send.at[me], hid_ref.at[me], load_sems.at[2])
    stay.start()

    rinv = lax.rsqrt(jnp.sum(square, -1, keepdims=True) / width + NORM_EPS)
    headb = head[...].astype(BF16)
    heads = jnp.zeros((rows, LANES), F32)
    for j, cut in enumerate(tiles):
        hb = (hidden[:, cut] * rinv).astype(BF16)
        hnorm[:, cut] = hb
        heads = heads + lax.dot_general(
            hb, headb[:, j * tile : (j + 1) * tile], (((1,), (1,)), ((), ())), preferred_element_type=F32
        )
    await_bytes(stats.at[pl.ds(0, n - 1)], stat_recv)
    sums = jnp.sum(stats[...], 0)
    mean_adv = sums[0:1, 0:1] / total_rows
    var_adv = sums[0:1, 1:2] / total_rows - mean_adv * mean_adv
    advant = ((cols[0, :, 0:1] - mean_adv) * lax.rsqrt(var_adv + NORM_EPS)).astype(BF16).astype(F32)
    ret = cols[1, :, 0:1].astype(BF16).astype(F32)
    lane = lax.broadcasted_iota(jnp.int32, (1, LANES), 1)
    one = lax.rem(lane, 16)
    first = lane < 16
    is_act = (one < nact) & (lane < 32)
    is_value = (one == nact) & (lane < 32)
    inv = jnp.where(is_act, jnp.exp(-lstd[0:1, :]), 0.0)
    noise = cols[3]
    u = (cols[2] - heads) * inv
    logr = jnp.sum(jnp.where(first, -noise * u - 0.5 * u * u, 0.0), -1, keepdims=True)
    ratio = jnp.exp(logr)
    scale = 1.0 / jnp.sqrt(jnp.full((1, 1), total_rows, F32))
    clipped = jnp.clip(ratio, 1.0 - CLIP_EPS, 1.0 + CLIP_EPS)
    active = ratio * advant <= clipped * advant
    glogr = jnp.where(active, -scale * advant, 0.0) * ratio
    ghead = jnp.where(is_value, scale * (heads - ret), glogr * (inv * (noise + u)))
    std_part = jnp.sum(glogr * (noise * u + u * u), 0, keepdims=True)
    along = jnp.sum(jnp.where(first, ghead * heads, 0.0), -1, keepdims=True) / width
    pull = rinv * rinv * along

    def two_parts(value):
        high = value.astype(BF16)
        return jnp.where(first, high.astype(F32), value - high.astype(F32)).astype(BF16)

    gscaled = two_parts(ghead * rinv)
    for j, cut in enumerate(tiles):
        g = jnp.dot(gscaled, headb[:, j * tile : (j + 1) * tile], preferred_element_type=F32)
        ghid[:, cut] = (g - hidden[:, cut] * pull).astype(BF16)

    turns = 2 * jnp.minimum(p.row, L - 1 - p.row)
    up_first = 2 * p.row < L

    def goes_up(k):
        first = (k >= turns) | (lax.rem(k, 2) == 0)
        return (k < L - 1) & (first == up_first)

    def target(k):
        at = jnp.where(k < turns, k // 2, k - turns // 2)
        return jnp.where(goes_up(k), L - 1 - at, jnp.where(k < L - 1, at, p.row))

    zw = zq_in.shape[3]
    yw = width - zw
    y_cuts = [pl.ds(*c) for c in cuts_of(0, yw, 3)]
    z_cuts = [pl.ds(*c) for c in cuts_of(yw, zw, 2)]
    z_local = [pl.ds(*c) for c in cuts_of(0, zw, 2)]
    ny = len(y_cuts)

    def sib_copy(slot, j):
        cut = (y_cuts + z_cuts)[j]
        return remote(
            sib_out.at[slot, :, cut], sib_in.at[slot, :, cut], rs_sib_send, rs_sib_recv.at[slot, j], sibling
        )

    def y_copy(k, j):
        return remote(
            y_out.at[k, :, y_cuts[j]], y_in.at[k, :, y_cuts[j]], y_send, y_recv.at[k, j], across
        )

    def yq_copy(j):
        return remote(yq_out.at[:, z_local[j]], yq_in.at[:, z_local[j]], yq_send, yq_recv.at[j], across)

    def contribute(k):
        rows_at = pl.ds(pl.multiple_of(target(k) * 4 * shard, 4 * shard), 4 * shard)

        def share(cross, core):
            line = (1 - p.col) if cross else p.col
            return pl.ds(pl.multiple_of((line * 2 + core) * shard, shard), shard)

        for j, cut in enumerate(y_cuts + z_cuts):
            layer[:, cut] = jnp.dot(normed_t[rows_at], ghid[:, cut], preferred_element_type=F32)
            for cross in (1, 0):
                sib_out[2 * k + cross, :, cut] = layer[share(cross, 1 - p.core), cut].astype(BF16)
                sib_copy(2 * k + cross, j).start()
        for cut in y_cuts:
            own[k, :, cut] = layer[share(0, p.core), cut]
        for cross in (1, 0):
            for cut, at in zip(z_cuts, z_local):
                ownz[k, cross, :, at] = layer[share(cross, p.core), cut]
        for j, cut in enumerate(y_cuts):
            sib_copy(2 * k + 1, j).wait_recv()
            y_out[k, :, cut] = (
                layer[share(1, p.core), cut] + sib_in[2 * k + 1, :, cut].astype(F32)
            ).astype(BF16)
            y_copy(k, j).start()

    def chip_sum(k, j):
        cut = y_cuts[j]
        sib_copy(2 * k, j).wait_recv()
        y_copy(k, j).wait_recv()
        return own[k, :, cut] + sib_in[2 * k, :, cut].astype(F32) + y_in[k, :, cut].astype(F32)

    def line_sum(k, j):
        for cross in range(2):
            sib_copy(2 * k + cross, ny + j).wait_recv()
            ownz[k, cross, :, z_local[j]] += sib_in[2 * k + cross, :, z_cuts[j]].astype(F32)

    def line_add(k, slot, j):
        zq_copy(0, slot, 0, j).wait_recv()
        for cross in range(2):
            ownz[k, cross, :, z_local[j]] += zq_in[slot, cross, :, z_local[j]].astype(F32)

    def zq_copy(to, slot, k, j):
        return remote(
            zq_out.at[k, :, :, z_local[j]], zq_in.at[slot, :, :, z_local[j]], zq_send, zq_recv.at[slot, j],
            {"fsdp": p.at(to, p.col, p.core)},
        )

    def z_copy(to, slot, k, j):
        return remote(
            z_out.at[k, :, y_cuts[j]], z_in.at[slot, :, y_cuts[j]], z_send, z_recv.at[slot, j],
            {"fsdp": p.at(to, p.col, p.core)},
        )

    def z_arrival(slot, j):
        return z_copy(0, slot, 0, j)

    contribute(0)
    other_line(0, x_part)

    gparts = two_parts(ghead)
    row = lax.broadcasted_iota(jnp.int32, (16, LANES), 0)
    for j, cut in enumerate(tiles):
        part_sum = lax.dot_general(gparts, hnorm[:, cut], (((0,), (0,)), ((), ())), preferred_element_type=F32)
        both = part_sum[0:16] + part_sum[16:32]
        for i in range(tile // LANES):
            head_blk[j * (tile // LANES) + i] = jnp.where(
                row == nact + 1, std_part, both[:, i * LANES : (i + 1) * LANES]
            )
    nb = head_all.shape[0]
    is_reducer = me < nb

    def when_reducer(go):
        if nb == n:
            go()
        else:
            pl.when(is_reducer)(go)

    def keep_block():
        head_in[me] = head_blk[me]

    when_reducer(keep_block)
    spread(nb, lambda peer: head_blk.at[peer], head_in, head_sems.at[0], head_sems.at[1])

    def reduce_heads():
        def go():
            await_bytes(head_in.at[pl.ds(0, n - 1)], head_sems.at[1])
            head_sum[...] = jnp.sum(head_in[...], 0)
            head_all[me] = head_sum[...]
            spread(n, lambda peer: head_sum, head_all, head_sems.at[2], head_sems.at[3])

        when_reducer(go)

    def chain(k):
        up = goes_up(k)
        has_in = jnp.where(up, p.row > 0, p.row < L - 1)
        to = jnp.where(up, p.row + 1, p.row - 1)
        slot = jnp.where((target(k) == to) & jnp.logical_not(up), L, target(k))
        return has_in, to, slot

    def whole_line(k):
        has_in, to, slot = chain(k)
        for j, at in enumerate(z_local):
            line_sum(k, j)

            @pl.when(has_in)
            def _():
                line_add(k, target(k), j)

            for cross in range(2):
                zq_out[k, cross, :, at] = ownz[k, cross, :, at].astype(BF16)
            zq_copy(to, slot, k, j).start()

    @pl.when(p.at_end)
    def _():
        whole_line(0)

    n_ext = ext_in.shape[0]
    rows_e = n_ext * slot_rows

    def early_rows():
        @pl.when(p.at_end)
        def _():
            await_bytes(ext_in.at[pl.ds(0, n_ext // 2)], ext_recv)

        @pl.when(jnp.logical_not(p.at_end))
        def _():
            await_bytes(ext_in, ext_recv)

        def early(cut):
            return ext_in[:, :, cut].astype(F32).reshape(rows_e, cut.size)

        square_e = jnp.zeros((rows_e, LANES), F32)
        for j in range(0, width, LANES):
            xf = early(pl.ds(j, LANES))
            square_e = square_e + xf * xf
        scale_e = lax.rsqrt(jnp.sum(square_e, -1, keepdims=True) / width + NORM_EPS)
        for cut in tiles:
            normed_e[:, cut] = (early(cut) * scale_e * gain_ref[:, cut]).astype(BF16)
        for cut in tiles:
            h = early(cut) + jnp.dot(normed_e[...], held[:, cut], preferred_element_type=F32)
            ext_out[:, :, cut] = h.astype(BF16).reshape(n_ext, slot_rows, tile)
        for end in range(2):
            @pl.when(p.row != end * (L - 1))
            def _():
                for core in range(2):
                    source = p.at(end * (L - 1), p.col, core)
                    slot = (end * 2 + core) * 2
                    hid_ref[source] = ext_out[slot]
                    remote(ext_out.at[slot + 1], hid_ref.at[source], fwd_send, a2a_recv, across).start()

    def pass_on(k):
        t = target(k)
        has_in, to, slot = chain(k)

        @pl.when(jnp.logical_not(p.at_end))
        def _():
            whole_line(k)

        for j, cut in enumerate(y_cuts):
            own[k, :, cut] = chip_sum(k, j)

            @pl.when(has_in)
            def _():
                z_arrival(t, j).wait_recv()
                own[k, :, cut] += z_in[t, :, cut].astype(F32)

            z_out[k, :, cut] = own[k, :, cut].astype(BF16)
            z_copy(to, slot, k, j).start()

        @pl.when(k == 1)
        def _():
            reduce_heads()

    def rest_of(k, _):
        @pl.when(k == 1)
        def _():
            other_line(L - 1, ring_part)

        other_line(k, x_part)
        contribute(k)

        @pl.when(p.at_end & (k < L - 1))
        def _():
            whole_line(k)

        @pl.when(k == min(2, L - 1))
        def _():
            early_rows()

        ready = jnp.where(p.at_end, k - 1, k - 2)

        @pl.when(ready >= 0)
        def _():
            pass_on(ready)

        return 0

    lax.fori_loop(1, L, rest_of, 0)

    @pl.when(jnp.logical_not(p.at_end))
    def _():
        pass_on(L - 2)

    for j, at in enumerate(z_local):
        line_sum(L - 1, j)

        @pl.when(p.row > 0)
        def _():
            line_add(L - 1, p.row, j)

        @pl.when(p.row < L - 1)
        def _():
            line_add(L - 1, L, j)

        yq_out[:, at] = ownz[L - 1, 1, :, at].astype(BF16)
        yq_copy(j).start()
    for j, cut in enumerate(y_cuts):
        grad_ref[:, cut] = chip_sum(L - 1, j)

        @pl.when(p.row > 0)
        def _():
            z_arrival(p.row, j).wait_recv()
            grad_ref[:, cut] += z_in[p.row, :, cut].astype(F32)

        @pl.when(p.row < L - 1)
        def _():
            z_arrival(L, j).wait_recv()
            grad_ref[:, cut] += z_in[L, :, cut].astype(F32)

    for j, (cut, at) in enumerate(zip(z_cuts, z_local)):
        yq_copy(j).wait_recv()
        grad_ref[:, cut] = ownz[L - 1, 0, :, at] + yq_in[:, at].astype(F32)

    if nb == n:
        await_bytes(head_all.at[pl.ds(0, nb - 1)], head_sems.at[3])
    else:
        @pl.when(is_reducer)
        def _():
            await_bytes(head_all.at[pl.ds(0, nb - 1)], head_sems.at[3])

        @pl.when(jnp.logical_not(is_reducer))
        def _():
            await_bytes(head_all.at[pl.ds(0, nb)], head_sems.at[3])

    for j in range(nb):
        headg_ref[:, j * LANES : (j + 1) * LANES] = head_all[j, 0 : nact + 1, :]
    stdg_ref[...] = head_all[0, nact + 1 : nact + 2, 0:nact]
    stay.wait()

    @pl.when(p.at_end)
    def _():
        await_bytes(hid_ref.at[pl.ds(0, n - 3)], a2a_recv)
        await_bytes(send.at[pl.ds(0, 3)], a2a_send)
        await_bytes(ext_out.at[pl.ds(0, 2)], fwd_send)
        await_bytes(obs_send.at[pl.ds(0, 4 * (L - 1))], ext_send)
        await_bytes(held.at[pl.ds(0, shard), pl.ds(0, width - xw)], z_ag_send)

    @pl.when(jnp.logical_not(p.at_end))
    def _():
        await_bytes(hid_ref.at[pl.ds(0, n - 5)], a2a_recv)
        await_bytes(send.at[pl.ds(0, n - 1)], a2a_send)
        await_bytes(ext_out.at[pl.ds(0, 4)], fwd_send)
        await_bytes(held.at[pl.ds(0, (L + 1) * shard), pl.ds(0, width - xw)], z_ag_send)

    await_bytes(held.at[pl.ds(0, L * shard), pl.ds(0, width - xw)], y_ag_send)
    await_bytes(held.at[pl.ds(0, (2 * L - 1) * shard), pl.ds(0, xw)], x_send)
    await_bytes(held.at[pl.ds(0, 2 * L * shard)], sib_send)
    await_bytes(stats.at[pl.ds(0, n - 1)], stat_send)
    if nb == n:
        await_bytes(head_blk.at[pl.ds(0, nb - 1)], head_sems.at[0])
        await_bytes(head_in.at[pl.ds(0, n - 1)], head_sems.at[2])
    else:
        @pl.when(is_reducer)
        def _():
            await_bytes(head_blk.at[pl.ds(0, nb - 1)], head_sems.at[0])
            await_bytes(head_in.at[pl.ds(0, n - 1)], head_sems.at[2])

        @pl.when(jnp.logical_not(is_reducer))
        def _():
            await_bytes(head_blk.at[pl.ds(0, nb)], head_sems.at[0])

    await_bytes(sib_out, rs_sib_send)
    await_bytes(y_out, y_send)
    await_bytes(z_out.at[pl.ds(0, L - 1)], z_send)
    await_bytes(zq_out.at[pl.ds(0, L - 1)], zq_send)
    await_bytes(yq_out, yq_send)


def store_kernel(a, b, c, d, a_out, b_out, c_out, d_out, sems):
    copies = [
        pltpu.make_async_copy(src, dst, sems.at[i])
        for i, (src, dst) in enumerate(((a, a_out), (b, b_out), (c, c_out), (d, d_out)))
    ]
    for copy in copies:
        copy.start()
    for copy in copies:
        copy.wait()


def local(
    obs_feat, reward, value_old, done, minibatch_perm, old_mean, noise, gain_in, out_weight, head_weight, log_std
):
    rows, width = obs_feat.shape
    n = lax.axis_size("fsdp")
    steps = reward.shape[1]
    n_env = reward.shape[0]
    nact = log_std.shape[0]
    shard = out_weight.shape[0]
    block = max(shard, LANES)
    per = rows // n
    slot_rows = -(-per // 8) * 8
    L = n // 4
    nb = min(n, width // LANES)
    zw = width // LANES * 4 // 16 * LANES
    yw = width - zw
    vmem = pl.BlockSpec(memory_space=pltpu.VMEM)
    hbm = pl.BlockSpec(memory_space=pl.ANY)
    sem = pltpu.SemaphoreType.DMA
    V = pltpu.VMEM
    hid, grad, headg, stdg = pl.pallas_call(
        functools.partial(kernel, n, steps),
        name="step",
        out_shape=(
            V((n, slot_rows, width), BF16),
            V((shard, width), F32),
            V((nact + 1, width), F32),
            V((1, nact), F32),
        ),
        in_specs=[hbm, hbm] + [vmem] * 9,
        out_specs=(vmem, vmem, vmem, vmem),
        scratch_shapes=[
            V((rows, width), BF16),
            V((width, width), BF16),
            V((width // block, rows, block), BF16),
            V((rows, width), F32),
            V((rows, width), BF16),
            V((rows, width), BF16),
            V((n * slot_rows, rows), BF16),
            V((n, slot_rows, width), BF16),
            V((LANES, rows), F32),
            V((4, rows, LANES), F32),
            V((4, n_env, LANES), F32),
            V((LANES, width), F32),
            V((8, LANES), F32),
            V((n, 8, LANES), F32),
            V((8, LANES), F32),
            V((nb, 16, LANES), F32),
            V((n, 16, LANES), F32),
            V((16, LANES), F32),
            V((nb, 16, LANES), F32),
            V((2 * L, shard, width), BF16),
            V((2 * L, shard, width), BF16),
            V((L, shard, yw), BF16),
            V((L, shard, yw), BF16),
            V((L, shard, yw), BF16),
            V((L + 1, shard, yw), BF16),
            V((L, 2, shard, zw), BF16),
            V((L + 1, 2, shard, zw), BF16),
            V((shard, zw), BF16),
            V((shard, zw), BF16),
            V((L, shard, yw), F32),
            V((L, 2, shard, zw), F32),
            V((width, rows), BF16),
            V((4 * shard, width), F32),
            V((n, slot_rows, width), BF16),
            V((8, slot_rows, width), BF16),
            V((8, slot_rows, width), BF16),
            V((8 * slot_rows, width), BF16),
            sem((3,)),
            sem(()),
            sem((L, 4)),
            sem(()),
            sem((L, 4)),
            sem(()),
            sem((2 * L, 2)),
            sem((2 * L, 4)),
            sem((2 * L, 2)),
            sem(()),
            sem(()),
            sem(()),
            sem(()),
            sem(()),
            sem(()),
            sem(()),
            sem(()),
            sem((4,)),
            sem(()),
            sem((2 * L, 5)),
            sem(()),
            sem((L, 3)),
            sem(()),
            sem((L + 1, 3)),
            sem(()),
            sem((L + 1, 2)),
            sem(()),
            sem((2,)),
        ],
        compiler_params=pltpu.CompilerParams(
            collective_id=0, has_side_effects=True, vmem_limit_bytes=58 << 20
        ),
        cost_estimate=pl.CostEstimate(
            flops=4 * rows * width * width, bytes_accessed=16 * rows * width, transcendentals=0
        ),
    )(
        obs_feat, out_weight, gain_in[None, :], reward, value_old, done, minibatch_perm,
        old_mean.T, noise.T, head_weight.T, log_std[None, :],
    )
    results = (hid, grad, headg, stdg)
    hid, grad, headg, stdg = pl.pallas_call(
        store_kernel,
        name="store",
        out_shape=tuple(jax.ShapeDtypeStruct(r.shape, r.dtype) for r in results),
        in_specs=[hbm] * 4,
        out_specs=(hbm,) * 4,
        scratch_shapes=[sem((4,))],
        compiler_params=pltpu.CompilerParams(vmem_limit_bytes=1 << 20),
    )(*results)
    hid = hid[:, :per].reshape(rows, width)
    return (hid, grad, headg.T, stdg[0])


def solution(mesh):
    both = P(("groups", "fsdp"), None)
    return jax.shard_map(
        local,
        mesh=mesh,
        in_specs=(
            both, both, both, both, P(("groups", "fsdp")), both, both, P(), P("fsdp", None), P(), P(),
        ),
        out_specs=(both, both, P("groups", None), P("groups")),
        check_vma=False,
    )
```

```python
import functools

import jax
import jax.numpy as jnp
from jax import lax
from jax.experimental import pallas as pl
from jax.experimental.pallas import tpu as pltpu
from jax.sharding import PartitionSpec as P

GAMMA = 0.99
LAMBDA_GAE = 0.95
CLIP_EPS = 0.2
NORM_EPS = 1e-05
MESH = pl.DeviceIdType.MESH
LANES = 128
F32 = jnp.float32
BF16 = jnp.bfloat16


class Place:
    def __init__(self, n):
        self.me = lax.axis_index("fsdp")
        self.group = lax.axis_index("groups")
        self.rows = n // 4
        self.core = lax.rem(self.me, 2)
        chip = self.me // 2
        self.col = lax.rem(chip, 2)
        self.row = chip // 2
        self.sibling = self.me + 1 - 2 * self.core
        self.across = self.at(self.row, 1 - self.col, self.core)
        self.at_end = (self.row == 0) | (self.row == self.rows - 1)

    def at(self, row, col, core):
        return (row * 2 + col) * 2 + core

    def nth_row(self, q):
        below, above = self.row, self.rows - 1 - self.row
        near = jnp.minimum(below, above)
        toward = jnp.where(below < above, 1, -1)
        inner = self.row + toward * jnp.where(lax.rem(q, 2) == 1, -((q + 1) // 2), q // 2)
        outer = self.row + toward * (q - near)
        return jnp.where(q <= 2 * near, inner, outer)


def remote(src, dst, send, recv, device):
    return pltpu.make_async_remote_copy(
        src_ref=src, dst_ref=dst, send_sem=send, recv_sem=recv, device_id=device, device_id_type=MESH
    )


def await_bytes(part, sem):
    pltpu.make_async_copy(part, part, sem).wait()


def cuts_of(start, size, count):
    blocks, cuts = size // LANES, []
    for i in range(count):
        take = -(-blocks // (count - i))
        cuts.append((start, take * LANES))
        start, blocks = start + take * LANES, blocks - take
    return cuts


def lanes(start, size):
    return pl.ds(pl.multiple_of(start, LANES), size)


def kernel(
    n, steps,
    x_hbm, w_hbm, gain_ref, reward_ref, value_ref, done_ref, perm_ref, mean_ref, noise_ref, head_ref, std_ref,
    hid_ref, grad_ref, headg_ref, stdg_ref,
    xv, held, normed, hidden, hnorm, ghid, place, send, rows_t, cols, envs, head, lstd,
    stats, stat_own, head_blk, head_in, head_sum, head_all,
    sib_out, sib_in, y_out, y_in, z_out, z_in, zq_out, zq_in, yq_out, yq_in, own, ownz, normed_t, layer,
    obs_send, ext_in, ext_out, normed_e,
    load_sems, z_ag_send, z_ag_recv, y_ag_send, y_ag_recv, x_send, x_recv, sibr_recv, sibx_recv, sib_send,
    ext_send, ext_recv, fwd_send,
    stat_send, stat_recv, a2a_send, a2a_recv, head_sems,
    rs_sib_send, rs_sib_recv, y_send, y_recv, z_send, z_recv, zq_send, zq_recv, yq_send, yq_recv,
):
    p = Place(n)
    me, L = p.me, p.rows
    rows, width = xv.shape
    shard = w_hbm.shape[0]
    block = normed.shape[2]
    whole_blocks = shard == block
    nact = mean_ref.shape[0]
    n_env = reward_ref.shape[0]
    slot_rows = send.shape[1]
    per = rows // n
    tile = width // 4
    tiles = [pl.ds(j * tile, tile) for j in range(4)]
    total_rows = rows * n

    load_x = pltpu.make_async_copy(x_hbm, xv, load_sems.at[0])
    load_x.start()
    load_w = pltpu.make_async_copy(w_hbm, held.at[pl.ds(pl.multiple_of(me * shard, shard), shard)], load_sems.at[1])
    load_w.start()

    ext_in[...] = jnp.zeros_like(ext_in)
    barrier = pltpu.get_barrier_semaphore()

    @pl.loop(1, n)
    def _(k):
        pl.semaphore_signal(barrier, inc=1, device_id={"fsdp": lax.rem(me + k, n)}, device_id_type=MESH)

    pl.semaphore_signal(barrier, inc=1, device_id={"groups": 1 - p.group}, device_id_type=MESH)

    perm = perm_ref[...].reshape(1, rows)
    slot_of = lax.div(perm, rows) * slot_rows + lax.rem(perm, per)
    place[...] = jnp.where(lax.broadcasted_iota(jnp.int32, place.shape, 0) == slot_of, 1.0, 0.0).astype(BF16)
    load_x.wait()

    @pl.when(p.at_end)
    def _():
        for cut in tiles:
            moved = jnp.dot(place[...], xv[:, cut], preferred_element_type=F32).astype(BF16)
            obs_send[:, :, cut] = moved.reshape(n, slot_rows, tile)

    pl.semaphore_wait(barrier, n)

    xw = width // LANES * 5 // 16 * LANES
    rest = width - 2 * xw
    ring_cuts = cuts_of(p.group * (width - xw), xw, 2) + cuts_of(xw, rest, 2)
    x_cuts = cuts_of((1 - p.group) * (width - xw), xw, 2)
    sibling = {"fsdp": p.sibling}
    partner = {"groups": 1 - p.group}
    across = {"fsdp": p.across}

    def owner(row, line, core):
        return p.at(row, p.col if line == 0 else 1 - p.col, core)

    def part(device, cut):
        return held.at[pl.ds(pl.multiple_of(device * shard, shard), shard), lanes(*cut)]

    def z_ag(o, i, to):
        ref = part(owner(o, 0, p.core), ring_cuts[i])
        return remote(ref, ref, z_ag_send, z_ag_recv.at[o, i], {"fsdp": p.at(to, p.col, p.core)})

    def y_ag(o, line, i):
        ref = part(owner(o, line, p.core), ring_cuts[i])
        return remote(ref, ref, y_ag_send, y_ag_recv.at[o, i], across)

    def x_ag(o, line, i, cuts):
        ref = part(owner(o, line, p.core), cuts[i])
        return remote(ref, ref, x_send, x_recv.at[2 * o + line, i], partner)

    def sibr(o, line, i, core):
        ref = part(owner(o, line, core), ring_cuts[i])
        return remote(ref, ref, sib_send, sibr_recv.at[2 * o + line, i], sibling)

    def sibx(o, line, i, core):
        ref = part(owner(o, line, core), x_cuts[i])
        return remote(ref, ref, sib_send, sibx_recv.at[2 * o + line, i], sibling)

    def ext_copies(to):
        for core in range(2):
            for kind in range(2):
                block_of = p.at(to, p.col if kind == 0 else 1 - p.col, core)
                slot = (jnp.where(p.row > 0, 2, 0) + p.core) * 2 + kind
                remote(
                    obs_send.at[block_of], ext_in.at[slot], ext_send, ext_recv,
                    {"fsdp": p.at(to, p.col, core)},
                ).start()

    load_w.wait()
    for i in range(4):
        @pl.when(p.row > 0)
        def _():
            z_ag(p.row, i, p.row - 1).start()

        @pl.when(p.row < L - 1)
        def _():
            z_ag(p.row, i, p.row + 1).start()

        y_ag(p.row, 0, i).start()
    for i in range(4):
        sibr(p.row, 0, i, p.core).start()
    for i in range(2):
        sibx(p.row, 0, i, p.core).start()

    @pl.when(p.at_end)
    def _():
        ext_copies(jnp.where(p.row > 0, p.row - 1, p.row + 1))

    square = jnp.zeros((rows, LANES), F32)
    for j in range(0, width, LANES):
        xf = xv[:, j : j + LANES].astype(F32)
        square = square + xf * xf
    scale_x = lax.rsqrt(jnp.sum(square, -1, keepdims=True) / width + NORM_EPS)
    for j in range(width // block):
        at = pl.ds(j * block, block)
        xf = xv[:, at].astype(F32)
        hidden[:, at] = xf
        normed[j] = (xf * scale_x * gain_ref[:, at]).astype(BF16)

    def add(index):
        for cut in tiles:
            hidden[:, cut] += jnp.dot(
                normed[index], held[pl.ds(pl.multiple_of(index * block, block), block), cut],
                preferred_element_type=F32,
            )

    def add_shard(device):
        if whole_blocks:
            add(device)

    def spread(count, source_of, dst, send_sem, recv_sem):
        @pl.loop(1, n)
        def _(k):
            peer = lax.rem(me + k, n)

            def go():
                remote(source_of(peer), dst.at[me], send_sem, recv_sem, {"fsdp": peer}).start()

            if count == n:
                go()
            else:
                pl.when(peer < count)(go)

    def advantages():
        lane = lax.broadcasted_iota(jnp.int32, (n_env, LANES), 1)
        envs[...] = jnp.zeros_like(envs)
        envs[0, :, 0:steps] = reward_ref[...]
        envs[1, :, 0 : steps + 1] = value_ref[...]
        envs[2, :, 0:steps] = 1.0 - done_ref[...].astype(F32)
        value, keep = envs[1], envs[2]
        ahead = pltpu.roll(value, LANES - 1, 1)
        gae = jnp.where(lane < steps, envs[0] + GAMMA * ahead * keep - value, 0.0)
        decay = GAMMA * LAMBDA_GAE * keep
        shift = 1
        while shift < steps:
            gae = gae + decay * pltpu.roll(gae, LANES - shift, 1)
            decay = decay * pltpu.roll(decay, LANES - shift, 1)
            shift *= 2
        envs[0] = gae
        envs[3] = gae + value
        spot = lax.broadcasted_iota(jnp.int32, (8, LANES), 1)
        stat_own[...] = jnp.where(spot == 0, jnp.sum(gae), jnp.where(spot == 1, jnp.sum(gae * gae), 0.0))
        stats[me] = stat_own[...]
        spread(n, lambda peer: stat_own, stats, stat_send, stat_recv)
        at_step = lax.broadcasted_iota(jnp.int32, (steps, LANES), 0) == lax.broadcasted_iota(
            jnp.int32, (steps, LANES), 1
        )
        for e in range(n_env):
            for c, k in ((0, 0), (1, 3)):
                line = jnp.broadcast_to(envs[k, e : e + 1, :], (steps, LANES))
                cols[c, e * steps : (e + 1) * steps, :] = jnp.broadcast_to(
                    jnp.sum(jnp.where(at_step, line, 0.0), -1, keepdims=True), (steps, LANES)
                )

    def columns():
        for k, ref in ((0, mean_ref), (1, noise_ref)):
            rows_t[...] = jnp.zeros_like(rows_t)
            rows_t[0:nact] = ref[...].astype(F32)
            rows_t[16 : 16 + nact] = ref[...].astype(F32)
            cols[2 + k] = jnp.transpose(rows_t[...])
        for j in range(width // block):
            normed_t[j * block : (j + 1) * block] = jnp.transpose(normed[j].astype(F32)).astype(BF16)
        head[...] = jnp.zeros_like(head)
        hf = head_ref[...].astype(F32)
        head[0 : nact + 1] = hf
        head[16 : 17 + nact] = hf
        lstd[...] = jnp.zeros_like(lstd)
        lstd[0:1, 0:nact] = std_ref[...]
        lstd[0:1, 16 : 16 + nact] = std_ref[...]

    def z_arrives(o):
        to = jnp.where(o < p.row, p.row + 1, p.row - 1)
        for i in range(4):
            z_ag(o, i, p.row).wait_recv()

            @pl.when((to >= 0) & (to < L))
            def _():
                z_ag(o, i, to).start()

            y_ag(o, 0, i).start()
            if i < 2:
                x_ag(o, 0, i, ring_cuts).start()
            sibr(o, 0, i, p.core).start()

    def y_arrives(o, pieces):
        for i in pieces:
            y_ag(o, 1, i).wait_recv()
            if i < 2:
                x_ag(o, 1, i, ring_cuts).start()
            sibr(o, 1, i, p.core).start()

    def x_arrives(o, line):
        for i in range(2):
            x_ag(o, line, i, x_cuts).wait_recv()
            sibx(o, line, i, p.core).start()

    def sib_arrives(o, line):
        for i in range(4):
            sibr(o, line, i, 1 - p.core).wait_recv()
        for i in range(2):
            sibx(o, line, i, 1 - p.core).wait_recv()

    def hop(q, _):
        z_arrives(p.nth_row(q))
        y_arrives(p.nth_row(q - 1), range(4))
        before = p.nth_row(q - 1)

        @pl.when(q > 1)
        def _():
            x_arrives(before, 0)

        add_shard(owner(before, 0, p.core))

        @pl.when(q == 1)
        def _():
            advantages()

        @pl.when((q > 1) & p.at_end)
        def _():
            ext_copies(jnp.where(p.row > 0, p.row - q, p.row + q))

        @pl.when(q == 2)
        def _():
            columns()

        @pl.when(q > 1)
        def _():
            o = p.nth_row(q - 2)
            x_arrives(o, 1)
            add_shard(owner(o, 1, p.core))
            sib_arrives(o, 0)
            add_shard(owner(o, 0, 1 - p.core))

        @pl.when(q > 2)
        def _():
            o = p.nth_row(q - 3)
            sib_arrives(o, 1)
            add_shard(owner(o, 1, 1 - p.core))

        return 0

    lax.fori_loop(1, L, hop, 0)

    def term(index, cut):
        rows_at = pl.ds(pl.multiple_of(index * block, block), block)
        return jnp.dot(normed[index], held[rows_at, lanes(*cut)], preferred_element_type=F32)

    far, farther, farthest = p.nth_row(L - 3), p.nth_row(L - 2), p.nth_row(L - 1)
    sib_arrives(farther, 0)
    add_shard(owner(farther, 0, 1 - p.core))
    sib_arrives(far, 1)
    add_shard(owner(far, 1, 1 - p.core))
    y_arrives(farthest, (0, 1))
    x_arrives(farthest, 0)
    add_shard(owner(farthest, 0, p.core))
    x_arrives(farther, 1)
    add_shard(owner(farther, 1, p.core))
    sib_arrives(farthest, 0)
    add_shard(owner(farthest, 0, 1 - p.core))
    sib_arrives(farther, 1)
    add_shard(owner(farther, 1, 1 - p.core))
    y_arrives(farthest, (2, 3))
    if whole_blocks:
        pair = (owner(farthest, 1, p.core), owner(farthest, 1, 1 - p.core))
    else:
        x_arrives(farthest, 1)
        sib_arrives(farthest, 1)
        lax.fori_loop(0, width // block - 2, lambda b, _: (add(b), 0)[1], 0)
        pair = (width // block - 2, width // block - 1)

    def finish(cut, square):
        h = hidden[:, lanes(*cut)] + term(pair[0], cut) + term(pair[1], cut)
        hidden[:, lanes(*cut)] = h
        for j in range(0, cut[1], LANES):
            piece = h[:, j : j + LANES]
            square = square + piece * piece
        moved = jnp.dot(place[...], h.astype(BF16), preferred_element_type=F32).astype(BF16)
        send[:, :, lanes(*cut)] = moved.reshape(n, slot_rows, cut[1])
        return square

    ring_part = (p.group * xw, width - xw)
    x_part = ((1 - p.group) * (width - xw), xw)

    def row_copy(peer, cut):
        return remote(
            send.at[peer, :, lanes(*cut)], hid_ref.at[me, :, lanes(*cut)], a2a_send, a2a_recv, {"fsdp": peer}
        )

    def same_line(cut):
        row_copy(p.sibling, cut).start()

        @pl.when(jnp.logical_not(p.at_end))
        def _():
            @pl.loop(1, L)
            def _(k):
                to = lax.rem(p.row + k, L)
                row_copy(p.at(to, p.col, 0), cut).start()
                row_copy(p.at(to, p.col, 1), cut).start()

    def other_line(m, cut):
        to = lax.rem(p.row + L // 2 + m, L)

        @pl.when(jnp.logical_not(p.at_end) | (to == p.row))
        def _():
            row_copy(p.at(to, 1 - p.col, 0), cut).start()
            row_copy(p.at(to, 1 - p.col, 1), cut).start()

    square = jnp.zeros((rows, LANES), F32)
    for i, cut in enumerate(ring_cuts):
        if whole_blocks:
            sibr(farthest, 1, i, 1 - p.core).wait_recv()
        square = finish(cut, square)

    @pl.loop(0, L)
    def _(m):
        other_line(m, ring_part)

    same_line(ring_part)
    if whole_blocks:
        x_arrives(farthest, 1)
    for i, cut in enumerate(x_cuts):
        if whole_blocks:
            sibx(farthest, 1, i, 1 - p.core).wait_recv()
        square = finish(cut, square)
    @pl.loop(0, L)
    def _(m):
        other_line(m, x_part)

    same_line(x_part)
    stay = pltpu.make_async_copy(send.at[me], hid_ref.at[me], load_sems.at[2])
    stay.start()

    rinv = lax.rsqrt(jnp.sum(square, -1, keepdims=True) / width + NORM_EPS)
    headb = head[...].astype(BF16)
    heads = jnp.zeros((rows, LANES), F32)
    for j, cut in enumerate(tiles):
        hb = (hidden[:, cut] * rinv).astype(BF16)
        hnorm[:, cut] = hb
        heads = heads + lax.dot_general(
            hb, headb[:, j * tile : (j + 1) * tile], (((1,), (1,)), ((), ())), preferred_element_type=F32
        )
    await_bytes(stats.at[pl.ds(0, n - 1)], stat_recv)
    sums = jnp.sum(stats[...], 0)
    mean_adv = sums[0:1, 0:1] / total_rows
    var_adv = sums[0:1, 1:2] / total_rows - mean_adv * mean_adv
    advant = ((cols[0, :, 0:1] - mean_adv) * lax.rsqrt(var_adv + NORM_EPS)).astype(BF16).astype(F32)
    ret = cols[1, :, 0:1].astype(BF16).astype(F32)
    lane = lax.broadcasted_iota(jnp.int32, (1, LANES), 1)
    one = lax.rem(lane, 16)
    first = lane < 16
    is_act = (one < nact) & (lane < 32)
    is_value = (one == nact) & (lane < 32)
    inv = jnp.where(is_act, jnp.exp(-lstd[0:1, :]), 0.0)
    noise = cols[3]
    u = (cols[2] - heads) * inv
    logr = jnp.sum(jnp.where(first, -noise * u - 0.5 * u * u, 0.0), -1, keepdims=True)
    ratio = jnp.exp(logr)
    scale = 1.0 / jnp.sqrt(jnp.full((1, 1), total_rows, F32))
    clipped = jnp.clip(ratio, 1.0 - CLIP_EPS, 1.0 + CLIP_EPS)
    active = ratio * advant <= clipped * advant
    glogr = jnp.where(active, -scale * advant, 0.0) * ratio
    ghead = jnp.where(is_value, scale * (heads - ret), glogr * (inv * (noise + u)))
    std_part = jnp.sum(glogr * (noise * u + u * u), 0, keepdims=True)
    along = jnp.sum(jnp.where(first, ghead * heads, 0.0), -1, keepdims=True) / width
    pull = rinv * rinv * along

    def two_parts(value):
        high = value.astype(BF16)
        return jnp.where(first, high.astype(F32), value - high.astype(F32)).astype(BF16)

    gscaled = two_parts(ghead * rinv)
    for j, cut in enumerate(tiles):
        g = jnp.dot(gscaled, headb[:, j * tile : (j + 1) * tile], preferred_element_type=F32)
        ghid[:, cut] = (g - hidden[:, cut] * pull).astype(BF16)

    turns = 2 * jnp.minimum(p.row, L - 1 - p.row)
    up_first = 2 * p.row < L

    def goes_up(k):
        first = (k >= turns) | (lax.rem(k, 2) == 0)
        return (k < L - 1) & (first == up_first)

    def target(k):
        at = jnp.where(k < turns, k // 2, k - turns // 2)
        return jnp.where(goes_up(k), L - 1 - at, jnp.where(k < L - 1, at, p.row))

    zw = zq_in.shape[3]
    yw = width - zw
    y_cuts = [pl.ds(*c) for c in cuts_of(0, yw, 3)]
    z_cuts = [pl.ds(*c) for c in cuts_of(yw, zw, 2)]
    z_local = [pl.ds(*c) for c in cuts_of(0, zw, 2)]
    ny = len(y_cuts)

    def sib_copy(slot, j):
        cut = (y_cuts + z_cuts)[j]
        return remote(
            sib_out.at[slot, :, cut], sib_in.at[slot, :, cut], rs_sib_send, rs_sib_recv.at[slot, j], sibling
        )

    def y_copy(k, j):
        return remote(
            y_out.at[k, :, y_cuts[j]], y_in.at[k, :, y_cuts[j]], y_send, y_recv.at[k, j], across
        )

    def yq_copy(j):
        return remote(yq_out.at[:, z_local[j]], yq_in.at[:, z_local[j]], yq_send, yq_recv.at[j], across)

    def contribute(k):
        rows_at = pl.ds(pl.multiple_of(target(k) * 4 * shard, 4 * shard), 4 * shard)

        def share(cross, core):
            line = (1 - p.col) if cross else p.col
            return pl.ds(pl.multiple_of((line * 2 + core) * shard, shard), shard)

        for j, cut in enumerate(y_cuts + z_cuts):
            layer[:, cut] = jnp.dot(normed_t[rows_at], ghid[:, cut], preferred_element_type=F32)
            for cross in (1, 0):
                sib_out[2 * k + cross, :, cut] = layer[share(cross, 1 - p.core), cut].astype(BF16)
                sib_copy(2 * k + cross, j).start()
        for j, cut in enumerate(y_cuts):
            sib_copy(2 * k + 1, j).wait_recv()
            y_out[k, :, cut] = (
                layer[share(1, p.core), cut] + sib_in[2 * k + 1, :, cut].astype(F32)
            ).astype(BF16)
            y_copy(k, j).start()
        for cut in y_cuts:
            own[k, :, cut] = layer[share(0, p.core), cut]
        for cross in (1, 0):
            for cut, at in zip(z_cuts, z_local):
                ownz[k, cross, :, at] = layer[share(cross, p.core), cut]

    def chip_sum(k, j):
        cut = y_cuts[j]
        sib_copy(2 * k, j).wait_recv()
        y_copy(k, j).wait_recv()
        return own[k, :, cut] + sib_in[2 * k, :, cut].astype(F32) + y_in[k, :, cut].astype(F32)

    def line_sum(k, j):
        for cross in range(2):
            sib_copy(2 * k + cross, ny + j).wait_recv()
            ownz[k, cross, :, z_local[j]] += sib_in[2 * k + cross, :, z_cuts[j]].astype(F32)

    def line_add(k, slot, j):
        zq_copy(0, slot, 0, j).wait_recv()
        for cross in range(2):
            ownz[k, cross, :, z_local[j]] += zq_in[slot, cross, :, z_local[j]].astype(F32)

    def zq_copy(to, slot, k, j):
        return remote(
            zq_out.at[k, :, :, z_local[j]], zq_in.at[slot, :, :, z_local[j]], zq_send, zq_recv.at[slot, j],
            {"fsdp": p.at(to, p.col, p.core)},
        )

    def z_copy(to, slot, k, j):
        return remote(
            z_out.at[k, :, y_cuts[j]], z_in.at[slot, :, y_cuts[j]], z_send, z_recv.at[slot, j],
            {"fsdp": p.at(to, p.col, p.core)},
        )

    def z_arrival(slot, j):
        return z_copy(0, slot, 0, j)

    contribute(0)

    gparts = two_parts(ghead)
    row = lax.broadcasted_iota(jnp.int32, (16, LANES), 0)
    for j, cut in enumerate(tiles):
        part_sum = lax.dot_general(gparts, hnorm[:, cut], (((0,), (0,)), ((), ())), preferred_element_type=F32)
        both = part_sum[0:16] + part_sum[16:32]
        for i in range(tile // LANES):
            head_blk[j * (tile // LANES) + i] = jnp.where(
                row == nact + 1, std_part, both[:, i * LANES : (i + 1) * LANES]
            )
    nb = head_all.shape[0]
    is_reducer = me < nb

    def when_reducer(go):
        if nb == n:
            go()
        else:
            pl.when(is_reducer)(go)

    def keep_block():
        head_in[me] = head_blk[me]

    when_reducer(keep_block)
    spread(nb, lambda peer: head_blk.at[peer], head_in, head_sems.at[0], head_sems.at[1])

    def reduce_heads():
        def go():
            await_bytes(head_in.at[pl.ds(0, n - 1)], head_sems.at[1])
            head_sum[...] = jnp.sum(head_in[...], 0)
            head_all[me] = head_sum[...]
            spread(n, lambda peer: head_sum, head_all, head_sems.at[2], head_sems.at[3])

        when_reducer(go)

    def chain(k):
        up = goes_up(k)
        has_in = jnp.where(up, p.row > 0, p.row < L - 1)
        to = jnp.where(up, p.row + 1, p.row - 1)
        slot = jnp.where((target(k) == to) & jnp.logical_not(up), L, target(k))
        return has_in, to, slot

    def whole_line(k):
        has_in, to, slot = chain(k)
        for j, at in enumerate(z_local):
            line_sum(k, j)

            @pl.when(has_in)
            def _():
                line_add(k, target(k), j)

            for cross in range(2):
                zq_out[k, cross, :, at] = ownz[k, cross, :, at].astype(BF16)
            zq_copy(to, slot, k, j).start()

    @pl.when(p.at_end)
    def _():
        whole_line(0)

    n_ext = ext_in.shape[0]
    rows_e = n_ext * slot_rows

    def early_rows():
        @pl.when(p.at_end)
        def _():
            await_bytes(ext_in.at[pl.ds(0, n_ext // 2)], ext_recv)

        @pl.when(jnp.logical_not(p.at_end))
        def _():
            await_bytes(ext_in, ext_recv)

        def early(cut):
            return ext_in[:, :, cut].astype(F32).reshape(rows_e, cut.size)

        square_e = jnp.zeros((rows_e, LANES), F32)
        for j in range(0, width, LANES):
            xf = early(pl.ds(j, LANES))
            square_e = square_e + xf * xf
        scale_e = lax.rsqrt(jnp.sum(square_e, -1, keepdims=True) / width + NORM_EPS)
        for cut in tiles:
            normed_e[:, cut] = (early(cut) * scale_e * gain_ref[:, cut]).astype(BF16)
        for cut in tiles:
            h = early(cut) + jnp.dot(normed_e[...], held[:, cut], preferred_element_type=F32)
            ext_out[:, :, cut] = h.astype(BF16).reshape(n_ext, slot_rows, tile)
        for end in range(2):
            @pl.when(p.row != end * (L - 1))
            def _():
                for core in range(2):
                    source = p.at(end * (L - 1), p.col, core)
                    slot = (end * 2 + core) * 2
                    hid_ref[source] = ext_out[slot]
                    remote(ext_out.at[slot + 1], hid_ref.at[source], fwd_send, a2a_recv, across).start()

    def pass_on(k):
        t = target(k)
        has_in, to, slot = chain(k)

        @pl.when(jnp.logical_not(p.at_end))
        def _():
            whole_line(k)

        for j, cut in enumerate(y_cuts):
            own[k, :, cut] = chip_sum(k, j)

            @pl.when(has_in)
            def _():
                z_arrival(t, j).wait_recv()
                own[k, :, cut] += z_in[t, :, cut].astype(F32)

            z_out[k, :, cut] = own[k, :, cut].astype(BF16)
            z_copy(to, slot, k, j).start()

        @pl.when(k == 1)
        def _():
            reduce_heads()

    def rest_of(k, _):
        contribute(k)

        @pl.when(p.at_end & (k < L - 1))
        def _():
            whole_line(k)

        @pl.when(k == min(2, L - 1))
        def _():
            early_rows()

        ready = jnp.where(p.at_end, k - 1, k - 2)

        @pl.when(ready >= 0)
        def _():
            pass_on(ready)

        return 0

    lax.fori_loop(1, L, rest_of, 0)

    @pl.when(jnp.logical_not(p.at_end))
    def _():
        pass_on(L - 2)

    for j, at in enumerate(z_local):
        line_sum(L - 1, j)

        @pl.when(p.row > 0)
        def _():
            line_add(L - 1, p.row, j)

        @pl.when(p.row < L - 1)
        def _():
            line_add(L - 1, L, j)

        yq_out[:, at] = ownz[L - 1, 1, :, at].astype(BF16)
        yq_copy(j).start()
    for j, cut in enumerate(y_cuts):
        grad_ref[:, cut] = chip_sum(L - 1, j)

        @pl.when(p.row > 0)
        def _():
            z_arrival(p.row, j).wait_recv()
            grad_ref[:, cut] += z_in[p.row, :, cut].astype(F32)

        @pl.when(p.row < L - 1)
        def _():
            z_arrival(L, j).wait_recv()
            grad_ref[:, cut] += z_in[L, :, cut].astype(F32)

    for j, (cut, at) in enumerate(zip(z_cuts, z_local)):
        yq_copy(j).wait_recv()
        grad_ref[:, cut] = ownz[L - 1, 0, :, at] + yq_in[:, at].astype(F32)

    if nb == n:
        await_bytes(head_all.at[pl.ds(0, nb - 1)], head_sems.at[3])
    else:
        @pl.when(is_reducer)
        def _():
            await_bytes(head_all.at[pl.ds(0, nb - 1)], head_sems.at[3])

        @pl.when(jnp.logical_not(is_reducer))
        def _():
            await_bytes(head_all.at[pl.ds(0, nb)], head_sems.at[3])

    for j in range(nb):
        headg_ref[:, j * LANES : (j + 1) * LANES] = head_all[j, 0 : nact + 1, :]
    stdg_ref[...] = head_all[0, nact + 1 : nact + 2, 0:nact]
    stay.wait()

    @pl.when(p.at_end)
    def _():
        await_bytes(hid_ref.at[pl.ds(0, n - 3)], a2a_recv)
        await_bytes(send.at[pl.ds(0, 3)], a2a_send)
        await_bytes(ext_out.at[pl.ds(0, 2)], fwd_send)
        await_bytes(obs_send.at[pl.ds(0, 4 * (L - 1))], ext_send)
        await_bytes(held.at[pl.ds(0, shard), pl.ds(0, width - xw)], z_ag_send)

    @pl.when(jnp.logical_not(p.at_end))
    def _():
        await_bytes(hid_ref.at[pl.ds(0, n - 5)], a2a_recv)
        await_bytes(send.at[pl.ds(0, n - 1)], a2a_send)
        await_bytes(ext_out.at[pl.ds(0, 4)], fwd_send)
        await_bytes(held.at[pl.ds(0, (L + 1) * shard), pl.ds(0, width - xw)], z_ag_send)

    await_bytes(held.at[pl.ds(0, L * shard), pl.ds(0, width - xw)], y_ag_send)
    await_bytes(held.at[pl.ds(0, (2 * L - 1) * shard), pl.ds(0, xw)], x_send)
    await_bytes(held.at[pl.ds(0, 2 * L * shard)], sib_send)
    await_bytes(stats.at[pl.ds(0, n - 1)], stat_send)
    if nb == n:
        await_bytes(head_blk.at[pl.ds(0, nb - 1)], head_sems.at[0])
        await_bytes(head_in.at[pl.ds(0, n - 1)], head_sems.at[2])
    else:
        @pl.when(is_reducer)
        def _():
            await_bytes(head_blk.at[pl.ds(0, nb - 1)], head_sems.at[0])
            await_bytes(head_in.at[pl.ds(0, n - 1)], head_sems.at[2])

        @pl.when(jnp.logical_not(is_reducer))
        def _():
            await_bytes(head_blk.at[pl.ds(0, nb)], head_sems.at[0])

    await_bytes(sib_out, rs_sib_send)
    await_bytes(y_out, y_send)
    await_bytes(z_out.at[pl.ds(0, L - 1)], z_send)
    await_bytes(zq_out.at[pl.ds(0, L - 1)], zq_send)
    await_bytes(yq_out, yq_send)


def store_kernel(a, b, c, d, a_out, b_out, c_out, d_out, sems):
    copies = [
        pltpu.make_async_copy(src, dst, sems.at[i])
        for i, (src, dst) in enumerate(((a, a_out), (b, b_out), (c, c_out), (d, d_out)))
    ]
    for copy in copies:
        copy.start()
    for copy in copies:
        copy.wait()


def local(
    obs_feat, reward, value_old, done, minibatch_perm, old_mean, noise, gain_in, out_weight, head_weight, log_std
):
    rows, width = obs_feat.shape
    n = lax.axis_size("fsdp")
    steps = reward.shape[1]
    n_env = reward.shape[0]
    nact = log_std.shape[0]
    shard = out_weight.shape[0]
    block = max(shard, LANES)
    per = rows // n
    slot_rows = -(-per // 8) * 8
    L = n // 4
    nb = min(n, width // LANES)
    zw = width // LANES * 4 // 16 * LANES
    yw = width - zw
    vmem = pl.BlockSpec(memory_space=pltpu.VMEM)
    hbm = pl.BlockSpec(memory_space=pl.ANY)
    sem = pltpu.SemaphoreType.DMA
    V = pltpu.VMEM
    hid, grad, headg, stdg = pl.pallas_call(
        functools.partial(kernel, n, steps),
        name="step",
        out_shape=(
            V((n, slot_rows, width), BF16),
            V((shard, width), F32),
            V((nact + 1, width), F32),
            V((1, nact), F32),
        ),
        in_specs=[hbm, hbm] + [vmem] * 9,
        out_specs=(vmem, vmem, vmem, vmem),
        scratch_shapes=[
            V((rows, width), BF16),
            V((width, width), BF16),
            V((width // block, rows, block), BF16),
            V((rows, width), F32),
            V((rows, width), BF16),
            V((rows, width), BF16),
            V((n * slot_rows, rows), BF16),
            V((n, slot_rows, width), BF16),
            V((LANES, rows), F32),
            V((4, rows, LANES), F32),
            V((4, n_env, LANES), F32),
            V((LANES, width), F32),
            V((8, LANES), F32),
            V((n, 8, LANES), F32),
            V((8, LANES), F32),
            V((nb, 16, LANES), F32),
            V((n, 16, LANES), F32),
            V((16, LANES), F32),
            V((nb, 16, LANES), F32),
            V((2 * L, shard, width), BF16),
            V((2 * L, shard, width), BF16),
            V((L, shard, yw), BF16),
            V((L, shard, yw), BF16),
            V((L, shard, yw), BF16),
            V((L + 1, shard, yw), BF16),
            V((L, 2, shard, zw), BF16),
            V((L + 1, 2, shard, zw), BF16),
            V((shard, zw), BF16),
            V((shard, zw), BF16),
            V((L, shard, yw), F32),
            V((L, 2, shard, zw), F32),
            V((width, rows), BF16),
            V((4 * shard, width), F32),
            V((n, slot_rows, width), BF16),
            V((8, slot_rows, width), BF16),
            V((8, slot_rows, width), BF16),
            V((8 * slot_rows, width), BF16),
            sem((3,)),
            sem(()),
            sem((L, 4)),
            sem(()),
            sem((L, 4)),
            sem(()),
            sem((2 * L, 2)),
            sem((2 * L, 4)),
            sem((2 * L, 2)),
            sem(()),
            sem(()),
            sem(()),
            sem(()),
            sem(()),
            sem(()),
            sem(()),
            sem(()),
            sem((4,)),
            sem(()),
            sem((2 * L, 5)),
            sem(()),
            sem((L, 3)),
            sem(()),
            sem((L + 1, 3)),
            sem(()),
            sem((L + 1, 2)),
            sem(()),
            sem((2,)),
        ],
        compiler_params=pltpu.CompilerParams(
            collective_id=0, has_side_effects=True, vmem_limit_bytes=58 << 20
        ),
        cost_estimate=pl.CostEstimate(
            flops=4 * rows * width * width, bytes_accessed=16 * rows * width, transcendentals=0
        ),
    )(
        obs_feat, out_weight, gain_in[None, :], reward, value_old, done, minibatch_perm,
        old_mean.T, noise.T, head_weight.T, log_std[None, :],
    )
    results = (hid, grad, headg, stdg)
    hid, grad, headg, stdg = pl.pallas_call(
        store_kernel,
        name="store",
        out_shape=tuple(jax.ShapeDtypeStruct(r.shape, r.dtype) for r in results),
        in_specs=[hbm] * 4,
        out_specs=(hbm,) * 4,
        scratch_shapes=[sem((4,))],
        compiler_params=pltpu.CompilerParams(vmem_limit_bytes=1 << 20),
    )(*results)
    hid = hid[:, :per].reshape(rows, width)
    return (hid, grad, headg.T, stdg[0])


def solution(mesh):
    both = P(("groups", "fsdp"), None)
    return jax.shard_map(
        local,
        mesh=mesh,
        in_specs=(
            both, both, both, both, P(("groups", "fsdp")), both, both, P(), P("fsdp", None), P(), P(),
        ),
        out_specs=(both, both, P("groups", None), P("groups")),
        check_vma=False,
    )
```

```python
import functools

import jax
import jax.numpy as jnp
from jax import lax
from jax.experimental import pallas as pl
from jax.experimental.pallas import tpu as pltpu
from jax.sharding import PartitionSpec as P

GAMMA = 0.99
LAMBDA_GAE = 0.95
CLIP_EPS = 0.2
NORM_EPS = 1e-05
MESH = pl.DeviceIdType.MESH
LANES = 128
F32 = jnp.float32
BF16 = jnp.bfloat16


class Place:
    def __init__(self, n):
        self.me = lax.axis_index("fsdp")
        self.group = lax.axis_index("groups")
        self.rows = n // 4
        self.core = lax.rem(self.me, 2)
        chip = self.me // 2
        self.col = lax.rem(chip, 2)
        self.row = chip // 2
        self.sibling = self.me + 1 - 2 * self.core
        self.across = self.at(self.row, 1 - self.col, self.core)
        self.at_end = (self.row == 0) | (self.row == self.rows - 1)

    def at(self, row, col, core):
        return (row * 2 + col) * 2 + core

    def nth_row(self, q):
        below, above = self.row, self.rows - 1 - self.row
        near = jnp.minimum(below, above)
        toward = jnp.where(below < above, 1, -1)
        inner = self.row + toward * jnp.where(lax.rem(q, 2) == 1, -((q + 1) // 2), q // 2)
        outer = self.row + toward * (q - near)
        return jnp.where(q <= 2 * near, inner, outer)


def remote(src, dst, send, recv, device):
    return pltpu.make_async_remote_copy(
        src_ref=src, dst_ref=dst, send_sem=send, recv_sem=recv, device_id=device, device_id_type=MESH
    )


def await_bytes(part, sem):
    pltpu.make_async_copy(part, part, sem).wait()


def cuts_of(start, size, count):
    blocks, cuts = size // LANES, []
    for i in range(count):
        take = -(-blocks // (count - i))
        cuts.append((start, take * LANES))
        start, blocks = start + take * LANES, blocks - take
    return cuts


def lanes(start, size):
    return pl.ds(pl.multiple_of(start, LANES), size)


def kernel(
    n, steps,
    x_hbm, w_hbm, gain_ref, reward_ref, value_ref, done_ref, perm_ref, mean_ref, noise_ref, head_ref, std_ref,
    hid_ref, grad_ref, headg_ref, stdg_ref,
    xv, held, normed, hidden, hnorm, ghid, place, send, rows_t, cols, envs, head, lstd,
    stats, stat_own, head_blk, head_in, head_sum, head_all,
    sib_out, sib_in, y_out, y_in, z_out, z_in, zq_out, zq_in, yq_out, yq_in, own, ownz, normed_t, layer,
    obs_send, ext_in, ext_out, normed_e,
    load_sems, z_ag_send, z_ag_recv, y_ag_send, y_ag_recv, x_send, x_recv, sibr_recv, sibx_recv, sib_send,
    ext_send, ext_recv, fwd_send,
    stat_send, stat_recv, a2a_send, a2a_recv, head_sems,
    rs_sib_send, rs_sib_recv, y_send, y_recv, z_send, z_recv, zq_send, zq_recv, yq_send, yq_recv,
):
    p = Place(n)
    me, L = p.me, p.rows
    rows, width = xv.shape
    shard = w_hbm.shape[0]
    block = normed.shape[2]
    whole_blocks = shard == block
    nact = mean_ref.shape[0]
    n_env = reward_ref.shape[0]
    slot_rows = send.shape[1]
    per = rows // n
    tile = width // 4
    tiles = [pl.ds(j * tile, tile) for j in range(4)]
    total_rows = rows * n

    load_x = pltpu.make_async_copy(x_hbm, xv, load_sems.at[0])
    load_x.start()
    load_w = pltpu.make_async_copy(w_hbm, held.at[pl.ds(pl.multiple_of(me * shard, shard), shard)], load_sems.at[1])
    load_w.start()

    ext_in[...] = jnp.zeros_like(ext_in)
    barrier = pltpu.get_barrier_semaphore()

    @pl.loop(1, n)
    def _(k):
        pl.semaphore_signal(barrier, inc=1, device_id={"fsdp": lax.rem(me + k, n)}, device_id_type=MESH)

    pl.semaphore_signal(barrier, inc=1, device_id={"groups": 1 - p.group}, device_id_type=MESH)

    perm = perm_ref[...].reshape(1, rows)
    slot_of = lax.div(perm, rows) * slot_rows + lax.rem(perm, per)
    place[...] = jnp.where(lax.broadcasted_iota(jnp.int32, place.shape, 0) == slot_of, 1.0, 0.0).astype(BF16)
    load_x.wait()

    @pl.when(p.at_end)
    def _():
        for cut in tiles:
            moved = jnp.dot(place[...], xv[:, cut], preferred_element_type=F32).astype(BF16)
            obs_send[:, :, cut] = moved.reshape(n, slot_rows, tile)

    pl.semaphore_wait(barrier, n)

    xw = width // LANES * 5 // 16 * LANES
    rest = width - 2 * xw
    ring_cuts = cuts_of(p.group * (width - xw), xw, 2) + cuts_of(xw, rest, 2)
    x_cuts = cuts_of((1 - p.group) * (width - xw), xw, 2)
    sibling = {"fsdp": p.sibling}
    partner = {"groups": 1 - p.group}
    across = {"fsdp": p.across}

    def owner(row, line, core):
        return p.at(row, p.col if line == 0 else 1 - p.col, core)

    def part(device, cut):
        return held.at[pl.ds(pl.multiple_of(device * shard, shard), shard), lanes(*cut)]

    def z_ag(o, i, to):
        ref = part(owner(o, 0, p.core), ring_cuts[i])
        return remote(ref, ref, z_ag_send, z_ag_recv.at[o, i], {"fsdp": p.at(to, p.col, p.core)})

    def y_ag(o, line, i):
        ref = part(owner(o, line, p.core), ring_cuts[i])
        return remote(ref, ref, y_ag_send, y_ag_recv.at[o, i], across)

    def x_ag(o, line, i, cuts):
        ref = part(owner(o, line, p.core), cuts[i])
        return remote(ref, ref, x_send, x_recv.at[2 * o + line, i], partner)

    def sibr(o, line, i, core):
        ref = part(owner(o, line, core), ring_cuts[i])
        return remote(ref, ref, sib_send, sibr_recv.at[2 * o + line, i], sibling)

    def sibx(o, line, i, core):
        ref = part(owner(o, line, core), x_cuts[i])
        return remote(ref, ref, sib_send, sibx_recv.at[2 * o + line, i], sibling)

    def ext_copies(to):
        for core in range(2):
            for kind in range(2):
                block_of = p.at(to, p.col if kind == 0 else 1 - p.col, core)
                slot = (jnp.where(p.row > 0, 2, 0) + p.core) * 2 + kind
                remote(
                    obs_send.at[block_of], ext_in.at[slot], ext_send, ext_recv,
                    {"fsdp": p.at(to, p.col, core)},
                ).start()

    load_w.wait()
    for i in range(4):
        @pl.when(p.row > 0)
        def _():
            z_ag(p.row, i, p.row - 1).start()

        @pl.when(p.row < L - 1)
        def _():
            z_ag(p.row, i, p.row + 1).start()

        y_ag(p.row, 0, i).start()
    for i in range(4):
        sibr(p.row, 0, i, p.core).start()
    for i in range(2):
        sibx(p.row, 0, i, p.core).start()

    @pl.when(p.at_end)
    def _():
        ext_copies(jnp.where(p.row > 0, p.row - 1, p.row + 1))

    square = jnp.zeros((rows, LANES), F32)
    for j in range(0, width, LANES):
        xf = xv[:, j : j + LANES].astype(F32)
        square = square + xf * xf
    scale_x = lax.rsqrt(jnp.sum(square, -1, keepdims=True) / width + NORM_EPS)
    for j in range(width // block):
        at = pl.ds(j * block, block)
        xf = xv[:, at].astype(F32)
        hidden[:, at] = xf
        normed[j] = (xf * scale_x * gain_ref[:, at]).astype(BF16)

    def add(index):
        for cut in tiles:
            hidden[:, cut] += jnp.dot(
                normed[index], held[pl.ds(pl.multiple_of(index * block, block), block), cut],
                preferred_element_type=F32,
            )

    def add_shard(device):
        if whole_blocks:
            add(device)

    def spread(count, source_of, dst, send_sem, recv_sem):
        @pl.loop(1, n)
        def _(k):
            peer = lax.rem(me + k, n)

            def go():
                remote(source_of(peer), dst.at[me], send_sem, recv_sem, {"fsdp": peer}).start()

            if count == n:
                go()
            else:
                pl.when(peer < count)(go)

    def advantages():
        lane = lax.broadcasted_iota(jnp.int32, (n_env, LANES), 1)
        envs[...] = jnp.zeros_like(envs)
        envs[0, :, 0:steps] = reward_ref[...]
        envs[1, :, 0 : steps + 1] = value_ref[...]
        envs[2, :, 0:steps] = 1.0 - done_ref[...].astype(F32)
        value, keep = envs[1], envs[2]
        ahead = pltpu.roll(value, LANES - 1, 1)
        gae = jnp.where(lane < steps, envs[0] + GAMMA * ahead * keep - value, 0.0)
        decay = GAMMA * LAMBDA_GAE * keep
        shift = 1
        while shift < steps:
            gae = gae + decay * pltpu.roll(gae, LANES - shift, 1)
            decay = decay * pltpu.roll(decay, LANES - shift, 1)
            shift *= 2
        envs[0] = gae
        envs[3] = gae + value
        spot = lax.broadcasted_iota(jnp.int32, (8, LANES), 1)
        stat_own[...] = jnp.where(spot == 0, jnp.sum(gae), jnp.where(spot == 1, jnp.sum(gae * gae), 0.0))
        stats[me] = stat_own[...]
        spread(n, lambda peer: stat_own, stats, stat_send, stat_recv)
        at_step = lax.broadcasted_iota(jnp.int32, (steps, LANES), 0) == lax.broadcasted_iota(
            jnp.int32, (steps, LANES), 1
        )
        for e in range(n_env):
            for c, k in ((0, 0), (1, 3)):
                line = jnp.broadcast_to(envs[k, e : e + 1, :], (steps, LANES))
                cols[c, e * steps : (e + 1) * steps, :] = jnp.broadcast_to(
                    jnp.sum(jnp.where(at_step, line, 0.0), -1, keepdims=True), (steps, LANES)
                )

    def columns():
        for k, ref in ((0, mean_ref), (1, noise_ref)):
            rows_t[...] = jnp.zeros_like(rows_t)
            rows_t[0:nact] = ref[...].astype(F32)
            rows_t[16 : 16 + nact] = ref[...].astype(F32)
            cols[2 + k] = jnp.transpose(rows_t[...])
        for j in range(width // block):
            normed_t[j * block : (j + 1) * block] = jnp.transpose(normed[j].astype(F32)).astype(BF16)
        head[...] = jnp.zeros_like(head)
        hf = head_ref[...].astype(F32)
        head[0 : nact + 1] = hf
        head[16 : 17 + nact] = hf
        lstd[...] = jnp.zeros_like(lstd)
        lstd[0:1, 0:nact] = std_ref[...]
        lstd[0:1, 16 : 16 + nact] = std_ref[...]

    def z_arrives(o):
        to = jnp.where(o < p.row, p.row + 1, p.row - 1)
        for i in range(4):
            z_ag(o, i, p.row).wait_recv()

            @pl.when((to >= 0) & (to < L))
            def _():
                z_ag(o, i, to).start()

            y_ag(o, 0, i).start()
            if i < 2:
                x_ag(o, 0, i, ring_cuts).start()
            sibr(o, 0, i, p.core).start()

    def y_arrives(o, pieces):
        for i in pieces:
            y_ag(o, 1, i).wait_recv()
            if i < 2:
                x_ag(o, 1, i, ring_cuts).start()
            sibr(o, 1, i, p.core).start()

    def x_arrives(o, line):
        for i in range(2):
            x_ag(o, line, i, x_cuts).wait_recv()
            sibx(o, line, i, p.core).start()

    def sib_arrives(o, line):
        for i in range(4):
            sibr(o, line, i, 1 - p.core).wait_recv()
        for i in range(2):
            sibx(o, line, i, 1 - p.core).wait_recv()

    def hop(q, _):
        z_arrives(p.nth_row(q))
        y_arrives(p.nth_row(q - 1), range(4))
        before = p.nth_row(q - 1)

        @pl.when(q > 1)
        def _():
            x_arrives(before, 0)

        add_shard(owner(before, 0, p.core))

        @pl.when(q == 1)
        def _():
            advantages()

        @pl.when((q > 1) & p.at_end)
        def _():
            ext_copies(jnp.where(p.row > 0, p.row - q, p.row + q))

        @pl.when(q == 2)
        def _():
            columns()

        @pl.when(q > 1)
        def _():
            o = p.nth_row(q - 2)
            x_arrives(o, 1)
            add_shard(owner(o, 1, p.core))
            sib_arrives(o, 0)
            add_shard(owner(o, 0, 1 - p.core))

        @pl.when(q > 2)
        def _():
            o = p.nth_row(q - 3)
            sib_arrives(o, 1)
            add_shard(owner(o, 1, 1 - p.core))

        return 0

    lax.fori_loop(1, L, hop, 0)

    def term(index, cut):
        rows_at = pl.ds(pl.multiple_of(index * block, block), block)
        return jnp.dot(normed[index], held[rows_at, lanes(*cut)], preferred_element_type=F32)

    far, farther, farthest = p.nth_row(L - 3), p.nth_row(L - 2), p.nth_row(L - 1)
    sib_arrives(farther, 0)
    add_shard(owner(farther, 0, 1 - p.core))
    sib_arrives(far, 1)
    add_shard(owner(far, 1, 1 - p.core))
    y_arrives(farthest, (0, 1))
    x_arrives(farthest, 0)
    add_shard(owner(farthest, 0, p.core))
    x_arrives(farther, 1)
    add_shard(owner(farther, 1, p.core))
    sib_arrives(farthest, 0)
    add_shard(owner(farthest, 0, 1 - p.core))
    sib_arrives(farther, 1)
    add_shard(owner(farther, 1, 1 - p.core))
    y_arrives(farthest, (2, 3))
    if whole_blocks:
        pair = (owner(farthest, 1, p.core), owner(farthest, 1, 1 - p.core))
    else:
        x_arrives(farthest, 1)
        sib_arrives(farthest, 1)
        lax.fori_loop(0, width // block - 2, lambda b, _: (add(b), 0)[1], 0)
        pair = (width // block - 2, width // block - 1)

    def finish(cut, square):
        h = hidden[:, lanes(*cut)] + term(pair[0], cut) + term(pair[1], cut)
        hidden[:, lanes(*cut)] = h
        for j in range(0, cut[1], LANES):
            piece = h[:, j : j + LANES]
            square = square + piece * piece
        moved = jnp.dot(place[...], h.astype(BF16), preferred_element_type=F32).astype(BF16)
        send[:, :, lanes(*cut)] = moved.reshape(n, slot_rows, cut[1])
        return square

    ring_part = (p.group * xw, width - xw)
    x_part = ((1 - p.group) * (width - xw), xw)

    def row_copy(peer, cut):
        return remote(
            send.at[peer, :, lanes(*cut)], hid_ref.at[me, :, lanes(*cut)], a2a_send, a2a_recv, {"fsdp": peer}
        )

    def same_line(cut):
        row_copy(p.sibling, cut).start()

        @pl.when(jnp.logical_not(p.at_end))
        def _():
            @pl.loop(1, L)
            def _(k):
                to = lax.rem(p.row + k, L)
                row_copy(p.at(to, p.col, 0), cut).start()
                row_copy(p.at(to, p.col, 1), cut).start()

    def other_line(m, cut):
        to = lax.rem(p.row + L // 2 + m, L)

        @pl.when(jnp.logical_not(p.at_end) | (to == p.row))
        def _():
            row_copy(p.at(to, 1 - p.col, 0), cut).start()
            row_copy(p.at(to, 1 - p.col, 1), cut).start()

    square = jnp.zeros((rows, LANES), F32)
    for i, cut in enumerate(ring_cuts):
        if whole_blocks:
            sibr(farthest, 1, i, 1 - p.core).wait_recv()
        square = finish(cut, square)

    @pl.loop(0, L)
    def _(m):
        other_line(m, ring_part)

    same_line(ring_part)
    if whole_blocks:
        x_arrives(farthest, 1)
    for i, cut in enumerate(x_cuts):
        if whole_blocks:
            sibx(farthest, 1, i, 1 - p.core).wait_recv()
        square = finish(cut, square)
    same_line(x_part)
    stay = pltpu.make_async_copy(send.at[me], hid_ref.at[me], load_sems.at[2])
    stay.start()

    rinv = lax.rsqrt(jnp.sum(square, -1, keepdims=True) / width + NORM_EPS)
    headb = head[...].astype(BF16)
    heads = jnp.zeros((rows, LANES), F32)
    for j, cut in enumerate(tiles):
        hb = (hidden[:, cut] * rinv).astype(BF16)
        hnorm[:, cut] = hb
        heads = heads + lax.dot_general(
            hb, headb[:, j * tile : (j + 1) * tile], (((1,), (1,)), ((), ())), preferred_element_type=F32
        )
    await_bytes(stats.at[pl.ds(0, n - 1)], stat_recv)
    sums = jnp.sum(stats[...], 0)
    mean_adv = sums[0:1, 0:1] / total_rows
    var_adv = sums[0:1, 1:2] / total_rows - mean_adv * mean_adv
    advant = ((cols[0, :, 0:1] - mean_adv) * lax.rsqrt(var_adv + NORM_EPS)).astype(BF16).astype(F32)
    ret = cols[1, :, 0:1].astype(BF16).astype(F32)
    lane = lax.broadcasted_iota(jnp.int32, (1, LANES), 1)
    one = lax.rem(lane, 16)
    first = lane < 16
    is_act = (one < nact) & (lane < 32)
    is_value = (one == nact) & (lane < 32)
    inv = jnp.where(is_act, jnp.exp(-lstd[0:1, :]), 0.0)
    noise = cols[3]
    u = (cols[2] - heads) * inv
    logr = jnp.sum(jnp.where(first, -noise * u - 0.5 * u * u, 0.0), -1, keepdims=True)
    ratio = jnp.exp(logr)
    scale = 1.0 / jnp.sqrt(jnp.full((1, 1), total_rows, F32))
    clipped = jnp.clip(ratio, 1.0 - CLIP_EPS, 1.0 + CLIP_EPS)
    active = ratio * advant <= clipped * advant
    glogr = jnp.where(active, -scale * advant, 0.0) * ratio
    ghead = jnp.where(is_value, scale * (heads - ret), glogr * (inv * (noise + u)))
    std_part = jnp.sum(glogr * (noise * u + u * u), 0, keepdims=True)
    along = jnp.sum(jnp.where(first, ghead * heads, 0.0), -1, keepdims=True) / width
    pull = rinv * rinv * along

    def two_parts(value):
        high = value.astype(BF16)
        return jnp.where(first, high.astype(F32), value - high.astype(F32)).astype(BF16)

    gscaled = two_parts(ghead * rinv)
    for j, cut in enumerate(tiles):
        g = jnp.dot(gscaled, headb[:, j * tile : (j + 1) * tile], preferred_element_type=F32)
        ghid[:, cut] = (g - hidden[:, cut] * pull).astype(BF16)

    turns = 2 * jnp.minimum(p.row, L - 1 - p.row)
    up_first = 2 * p.row < L

    def goes_up(k):
        first = (k >= turns) | (lax.rem(k, 2) == 0)
        return (k < L - 1) & (first == up_first)

    def target(k):
        at = jnp.where(k < turns, k // 2, k - turns // 2)
        return jnp.where(goes_up(k), L - 1 - at, jnp.where(k < L - 1, at, p.row))

    zw = zq_in.shape[3]
    yw = width - zw
    y_cuts = [pl.ds(*c) for c in cuts_of(0, yw, 3)]
    z_cuts = [pl.ds(*c) for c in cuts_of(yw, zw, 2)]
    z_local = [pl.ds(*c) for c in cuts_of(0, zw, 2)]
    ny = len(y_cuts)

    def sib_copy(slot, j):
        cut = (y_cuts + z_cuts)[j]
        return remote(
            sib_out.at[slot, :, cut], sib_in.at[slot, :, cut], rs_sib_send, rs_sib_recv.at[slot, j], sibling
        )

    def y_copy(k, j):
        return remote(
            y_out.at[k, :, y_cuts[j]], y_in.at[k, :, y_cuts[j]], y_send, y_recv.at[k, j], across
        )

    def yq_copy(j):
        return remote(yq_out.at[:, z_local[j]], yq_in.at[:, z_local[j]], yq_send, yq_recv.at[j], across)

    def contribute(k):
        rows_at = pl.ds(pl.multiple_of(target(k) * 4 * shard, 4 * shard), 4 * shard)

        def share(cross, core):
            line = (1 - p.col) if cross else p.col
            return pl.ds(pl.multiple_of((line * 2 + core) * shard, shard), shard)

        for j, cut in enumerate(y_cuts + z_cuts):
            layer[:, cut] = jnp.dot(normed_t[rows_at], ghid[:, cut], preferred_element_type=F32)
            for cross in (1, 0):
                sib_out[2 * k + cross, :, cut] = layer[share(cross, 1 - p.core), cut].astype(BF16)
                sib_copy(2 * k + cross, j).start()
        for j, cut in enumerate(y_cuts):
            sib_copy(2 * k + 1, j).wait_recv()
            y_out[k, :, cut] = (
                layer[share(1, p.core), cut] + sib_in[2 * k + 1, :, cut].astype(F32)
            ).astype(BF16)
            y_copy(k, j).start()
        for cut in y_cuts:
            own[k, :, cut] = layer[share(0, p.core), cut]
        for cross in (1, 0):
            for cut, at in zip(z_cuts, z_local):
                ownz[k, cross, :, at] = layer[share(cross, p.core), cut]

    def chip_sum(k, j):
        cut = y_cuts[j]
        sib_copy(2 * k, j).wait_recv()
        y_copy(k, j).wait_recv()
        return own[k, :, cut] + sib_in[2 * k, :, cut].astype(F32) + y_in[k, :, cut].astype(F32)

    def line_sum(k, j):
        for cross in range(2):
            sib_copy(2 * k + cross, ny + j).wait_recv()
            ownz[k, cross, :, z_local[j]] += sib_in[2 * k + cross, :, z_cuts[j]].astype(F32)

    def line_add(k, slot, j):
        zq_copy(0, slot, 0, j).wait_recv()
        for cross in range(2):
            ownz[k, cross, :, z_local[j]] += zq_in[slot, cross, :, z_local[j]].astype(F32)

    def zq_copy(to, slot, k, j):
        return remote(
            zq_out.at[k, :, :, z_local[j]], zq_in.at[slot, :, :, z_local[j]], zq_send, zq_recv.at[slot, j],
            {"fsdp": p.at(to, p.col, p.core)},
        )

    def z_copy(to, slot, k, j):
        return remote(
            z_out.at[k, :, y_cuts[j]], z_in.at[slot, :, y_cuts[j]], z_send, z_recv.at[slot, j],
            {"fsdp": p.at(to, p.col, p.core)},
        )

    def z_arrival(slot, j):
        return z_copy(0, slot, 0, j)

    contribute(0)

    @pl.loop(0, L)
    def _(m):
        other_line(m, x_part)


    gparts = two_parts(ghead)
    row = lax.broadcasted_iota(jnp.int32, (16, LANES), 0)
    for j, cut in enumerate(tiles):
        part_sum = lax.dot_general(gparts, hnorm[:, cut], (((0,), (0,)), ((), ())), preferred_element_type=F32)
        both = part_sum[0:16] + part_sum[16:32]
        for i in range(tile // LANES):
            head_blk[j * (tile // LANES) + i] = jnp.where(
                row == nact + 1, std_part, both[:, i * LANES : (i + 1) * LANES]
            )
    nb = head_all.shape[0]
    is_reducer = me < nb

    def when_reducer(go):
        if nb == n:
            go()
        else:
            pl.when(is_reducer)(go)

    def keep_block():
        head_in[me] = head_blk[me]

    when_reducer(keep_block)
    spread(nb, lambda peer: head_blk.at[peer], head_in, head_sems.at[0], head_sems.at[1])

    def reduce_heads():
        def go():
            await_bytes(head_in.at[pl.ds(0, n - 1)], head_sems.at[1])
            head_sum[...] = jnp.sum(head_in[...], 0)
            head_all[me] = head_sum[...]
            spread(n, lambda peer: head_sum, head_all, head_sems.at[2], head_sems.at[3])

        when_reducer(go)

    def chain(k):
        up = goes_up(k)
        has_in = jnp.where(up, p.row > 0, p.row < L - 1)
        to = jnp.where(up, p.row + 1, p.row - 1)
        slot = jnp.where((target(k) == to) & jnp.logical_not(up), L, target(k))
        return has_in, to, slot

    def whole_line(k):
        has_in, to, slot = chain(k)
        for j, at in enumerate(z_local):
            line_sum(k, j)

            @pl.when(has_in)
            def _():
                line_add(k, target(k), j)

            for cross in range(2):
                zq_out[k, cross, :, at] = ownz[k, cross, :, at].astype(BF16)
            zq_copy(to, slot, k, j).start()

    @pl.when(p.at_end)
    def _():
        whole_line(0)

    n_ext = ext_in.shape[0]
    rows_e = n_ext * slot_rows

    def early_rows():
        @pl.when(p.at_end)
        def _():
            await_bytes(ext_in.at[pl.ds(0, n_ext // 2)], ext_recv)

        @pl.when(jnp.logical_not(p.at_end))
        def _():
            await_bytes(ext_in, ext_recv)

        def early(cut):
            return ext_in[:, :, cut].astype(F32).reshape(rows_e, cut.size)

        square_e = jnp.zeros((rows_e, LANES), F32)
        for j in range(0, width, LANES):
            xf = early(pl.ds(j, LANES))
            square_e = square_e + xf * xf
        scale_e = lax.rsqrt(jnp.sum(square_e, -1, keepdims=True) / width + NORM_EPS)
        for cut in tiles:
            normed_e[:, cut] = (early(cut) * scale_e * gain_ref[:, cut]).astype(BF16)
        for cut in tiles:
            h = early(cut) + jnp.dot(normed_e[...], held[:, cut], preferred_element_type=F32)
            ext_out[:, :, cut] = h.astype(BF16).reshape(n_ext, slot_rows, tile)
        for end in range(2):
            @pl.when(p.row != end * (L - 1))
            def _():
                for core in range(2):
                    source = p.at(end * (L - 1), p.col, core)
                    slot = (end * 2 + core) * 2
                    hid_ref[source] = ext_out[slot]
                    remote(ext_out.at[slot + 1], hid_ref.at[source], fwd_send, a2a_recv, across).start()

    def pass_on(k):
        t = target(k)
        has_in, to, slot = chain(k)

        @pl.when(jnp.logical_not(p.at_end))
        def _():
            whole_line(k)

        for j, cut in enumerate(y_cuts):
            own[k, :, cut] = chip_sum(k, j)

            @pl.when(has_in)
            def _():
                z_arrival(t, j).wait_recv()
                own[k, :, cut] += z_in[t, :, cut].astype(F32)

            z_out[k, :, cut] = own[k, :, cut].astype(BF16)
            z_copy(to, slot, k, j).start()

        @pl.when(k == 1)
        def _():
            reduce_heads()

    def rest_of(k, _):
        contribute(k)

        @pl.when(p.at_end & (k < L - 1))
        def _():
            whole_line(k)

        @pl.when(k == min(2, L - 1))
        def _():
            early_rows()

        ready = jnp.where(p.at_end, k - 1, k - 2)

        @pl.when(ready >= 0)
        def _():
            pass_on(ready)

        return 0

    lax.fori_loop(1, L, rest_of, 0)

    @pl.when(jnp.logical_not(p.at_end))
    def _():
        pass_on(L - 2)

    for j, at in enumerate(z_local):
        line_sum(L - 1, j)

        @pl.when(p.row > 0)
        def _():
            line_add(L - 1, p.row, j)

        @pl.when(p.row < L - 1)
        def _():
            line_add(L - 1, L, j)

        yq_out[:, at] = ownz[L - 1, 1, :, at].astype(BF16)
        yq_copy(j).start()
    for j, cut in enumerate(y_cuts):
        grad_ref[:, cut] = chip_sum(L - 1, j)

        @pl.when(p.row > 0)
        def _():
            z_arrival(p.row, j).wait_recv()
            grad_ref[:, cut] += z_in[p.row, :, cut].astype(F32)

        @pl.when(p.row < L - 1)
        def _():
            z_arrival(L, j).wait_recv()
            grad_ref[:, cut] += z_in[L, :, cut].astype(F32)

    for j, (cut, at) in enumerate(zip(z_cuts, z_local)):
        yq_copy(j).wait_recv()
        grad_ref[:, cut] = ownz[L - 1, 0, :, at] + yq_in[:, at].astype(F32)

    if nb == n:
        await_bytes(head_all.at[pl.ds(0, nb - 1)], head_sems.at[3])
    else:
        @pl.when(is_reducer)
        def _():
            await_bytes(head_all.at[pl.ds(0, nb - 1)], head_sems.at[3])

        @pl.when(jnp.logical_not(is_reducer))
        def _():
            await_bytes(head_all.at[pl.ds(0, nb)], head_sems.at[3])

    for j in range(nb):
        headg_ref[:, j * LANES : (j + 1) * LANES] = head_all[j, 0 : nact + 1, :]
    stdg_ref[...] = head_all[0, nact + 1 : nact + 2, 0:nact]
    stay.wait()

    @pl.when(p.at_end)
    def _():
        await_bytes(hid_ref.at[pl.ds(0, n - 3)], a2a_recv)
        await_bytes(send.at[pl.ds(0, 3)], a2a_send)
        await_bytes(ext_out.at[pl.ds(0, 2)], fwd_send)
        await_bytes(obs_send.at[pl.ds(0, 4 * (L - 1))], ext_send)
        await_bytes(held.at[pl.ds(0, shard), pl.ds(0, width - xw)], z_ag_send)

    @pl.when(jnp.logical_not(p.at_end))
    def _():
        await_bytes(hid_ref.at[pl.ds(0, n - 5)], a2a_recv)
        await_bytes(send.at[pl.ds(0, n - 1)], a2a_send)
        await_bytes(ext_out.at[pl.ds(0, 4)], fwd_send)
        await_bytes(held.at[pl.ds(0, (L + 1) * shard), pl.ds(0, width - xw)], z_ag_send)

    await_bytes(held.at[pl.ds(0, L * shard), pl.ds(0, width - xw)], y_ag_send)
    await_bytes(held.at[pl.ds(0, (2 * L - 1) * shard), pl.ds(0, xw)], x_send)
    await_bytes(held.at[pl.ds(0, 2 * L * shard)], sib_send)
    await_bytes(stats.at[pl.ds(0, n - 1)], stat_send)
    if nb == n:
        await_bytes(head_blk.at[pl.ds(0, nb - 1)], head_sems.at[0])
        await_bytes(head_in.at[pl.ds(0, n - 1)], head_sems.at[2])
    else:
        @pl.when(is_reducer)
        def _():
            await_bytes(head_blk.at[pl.ds(0, nb - 1)], head_sems.at[0])
            await_bytes(head_in.at[pl.ds(0, n - 1)], head_sems.at[2])

        @pl.when(jnp.logical_not(is_reducer))
        def _():
            await_bytes(head_blk.at[pl.ds(0, nb)], head_sems.at[0])

    await_bytes(sib_out, rs_sib_send)
    await_bytes(y_out, y_send)
    await_bytes(z_out.at[pl.ds(0, L - 1)], z_send)
    await_bytes(zq_out.at[pl.ds(0, L - 1)], zq_send)
    await_bytes(yq_out, yq_send)


def store_kernel(a, b, c, d, a_out, b_out, c_out, d_out, sems):
    copies = [
        pltpu.make_async_copy(src, dst, sems.at[i])
        for i, (src, dst) in enumerate(((a, a_out), (b, b_out), (c, c_out), (d, d_out)))
    ]
    for copy in copies:
        copy.start()
    for copy in copies:
        copy.wait()


def local(
    obs_feat, reward, value_old, done, minibatch_perm, old_mean, noise, gain_in, out_weight, head_weight, log_std
):
    rows, width = obs_feat.shape
    n = lax.axis_size("fsdp")
    steps = reward.shape[1]
    n_env = reward.shape[0]
    nact = log_std.shape[0]
    shard = out_weight.shape[0]
    block = max(shard, LANES)
    per = rows // n
    slot_rows = -(-per // 8) * 8
    L = n // 4
    nb = min(n, width // LANES)
    zw = width // LANES * 4 // 16 * LANES
    yw = width - zw
    vmem = pl.BlockSpec(memory_space=pltpu.VMEM)
    hbm = pl.BlockSpec(memory_space=pl.ANY)
    sem = pltpu.SemaphoreType.DMA
    V = pltpu.VMEM
    hid, grad, headg, stdg = pl.pallas_call(
        functools.partial(kernel, n, steps),
        name="step",
        out_shape=(
            V((n, slot_rows, width), BF16),
            V((shard, width), F32),
            V((nact + 1, width), F32),
            V((1, nact), F32),
        ),
        in_specs=[hbm, hbm] + [vmem] * 9,
        out_specs=(vmem, vmem, vmem, vmem),
        scratch_shapes=[
            V((rows, width), BF16),
            V((width, width), BF16),
            V((width // block, rows, block), BF16),
            V((rows, width), F32),
            V((rows, width), BF16),
            V((rows, width), BF16),
            V((n * slot_rows, rows), BF16),
            V((n, slot_rows, width), BF16),
            V((LANES, rows), F32),
            V((4, rows, LANES), F32),
            V((4, n_env, LANES), F32),
            V((LANES, width), F32),
            V((8, LANES), F32),
            V((n, 8, LANES), F32),
            V((8, LANES), F32),
            V((nb, 16, LANES), F32),
            V((n, 16, LANES), F32),
            V((16, LANES), F32),
            V((nb, 16, LANES), F32),
            V((2 * L, shard, width), BF16),
            V((2 * L, shard, width), BF16),
            V((L, shard, yw), BF16),
            V((L, shard, yw), BF16),
            V((L, shard, yw), BF16),
            V((L + 1, shard, yw), BF16),
            V((L, 2, shard, zw), BF16),
            V((L + 1, 2, shard, zw), BF16),
            V((shard, zw), BF16),
            V((shard, zw), BF16),
            V((L, shard, yw), F32),
            V((L, 2, shard, zw), F32),
            V((width, rows), BF16),
            V((4 * shard, width), F32),
            V((n, slot_rows, width), BF16),
            V((8, slot_rows, width), BF16),
            V((8, slot_rows, width), BF16),
            V((8 * slot_rows, width), BF16),
            sem((3,)),
            sem(()),
            sem((L, 4)),
            sem(()),
            sem((L, 4)),
            sem(()),
            sem((2 * L, 2)),
            sem((2 * L, 4)),
            sem((2 * L, 2)),
            sem(()),
            sem(()),
            sem(()),
            sem(()),
            sem(()),
            sem(()),
            sem(()),
            sem(()),
            sem((4,)),
            sem(()),
            sem((2 * L, 5)),
            sem(()),
            sem((L, 3)),
            sem(()),
            sem((L + 1, 3)),
            sem(()),
            sem((L + 1, 2)),
            sem(()),
            sem((2,)),
        ],
        compiler_params=pltpu.CompilerParams(
            collective_id=0, has_side_effects=True, vmem_limit_bytes=58 << 20
        ),
        cost_estimate=pl.CostEstimate(
            flops=4 * rows * width * width, bytes_accessed=16 * rows * width, transcendentals=0
        ),
    )(
        obs_feat, out_weight, gain_in[None, :], reward, value_old, done, minibatch_perm,
        old_mean.T, noise.T, head_weight.T, log_std[None, :],
    )
    results = (hid, grad, headg, stdg)
    hid, grad, headg, stdg = pl.pallas_call(
        store_kernel,
        name="store",
        out_shape=tuple(jax.ShapeDtypeStruct(r.shape, r.dtype) for r in results),
        in_specs=[hbm] * 4,
        out_specs=(hbm,) * 4,
        scratch_shapes=[sem((4,))],
        compiler_params=pltpu.CompilerParams(vmem_limit_bytes=1 << 20),
    )(*results)
    hid = hid[:, :per].reshape(rows, width)
    return (hid, grad, headg.T, stdg[0])


def solution(mesh):
    both = P(("groups", "fsdp"), None)
    return jax.shard_map(
        local,
        mesh=mesh,
        in_specs=(
            both, both, both, both, P(("groups", "fsdp")), both, both, P(), P("fsdp", None), P(), P(),
        ),
        out_specs=(both, both, P("groups", None), P("groups")),
        check_vma=False,
    )
```
